512 devices in a mesh: tm: 128 (over x, z, core), space: 4 (over y).
Axes of the slice: x: 4, y: 4, z: 16, core: 2. Of those that a mesh axis runs over, the one named last changes fastest.
Arguments:
- guess: float32 [128, 1, 64, 4096], P('tm', None, None, 'space'), may hold values from -6 to 6
- kernels: bfloat16 [256, 64, 576], P('tm'), may hold values from -0.25 to 0.25
- biases: float32 [256, 64], P('tm'), may hold values from -6 to 6
- probes: bfloat16 [2, 1, 64, 4096], P(None, None, None, 'space'), may hold values from -6 to 6
Outputs:
- states: float32 [128, 1, 64, 4096], P('tm', None, None, 'space')
- log_change: float32 [256], P('tm')
The draws below stay inside these ranges and needn't reach their ends.
All inputs are finite; a program needn't handle non-finite values.
Results may differ from the reference program's by a relative error of at most 0.0018.
Values may be sent and summed in bfloat16 or wider, within the bound.
No kernel may reach another device: no remote copies, remote signals or barrier semaphores. Data moves between devices by JAX's collectives and lax.ppermute only.
A program may use at most 128 MiB of HBM per device.

```python
import jax
import jax.numpy as jnp
from jax import lax

CHANNELS = 64
WIDTH = 64
PROBES = 2
BATCH = 1
STEPS_DEV = 2
CELLS = 4096
GROUPS = 128
STEPS = 256
N_TM = 128


def block_levels(rng, extent, shards, least, top_value):
    factor_of = 1.0
    for dim, blocks in shards:
        steps = jax.random.uniform(jax.random.fold_in(jax.random.fold_in(rng, 6), dim), (blocks,), jnp.float32, least / len(shards), top_value / len(shards))
        factor_of = factor_of * jnp.repeat(jnp.exp(steps), extent[dim] // blocks).reshape((-1,) + (1,) * (len(extent) - 1 - dim))
    return factor_of


def normal_values(rng, extent, width, bound, shards=(), kind=jnp.bfloat16):
    result = width * jax.random.normal(rng, extent, jnp.float32)
    if shards:
        result = result * block_levels(rng, extent, shards, -0.22, 0.18)
    return jnp.clip(result, -bound, bound).astype(kind)


def setup_inputs(seed: int = 0) -> dict:
    key_list = jax.random.split(jax.random.key(seed), 5)
    return {
        "guess": normal_values(key_list[0], (GROUPS, BATCH, CHANNELS, CELLS), 1.0, 6.0, ((0, 128), (3, 4)), jnp.float32),
        "kernels": normal_values(key_list[1], (STEPS, CHANNELS, 9 * CHANNELS), (9 * CHANNELS) ** -0.5, 0.25, ((0, 128),)),
        "biases": normal_values(key_list[2], (STEPS, CHANNELS), 1.0, 6.0, ((0, 128),), jnp.float32),
        "probes": normal_values(key_list[3], (PROBES, BATCH, CHANNELS, CELLS), 1.0, 6.0, ((3, 4),)),
    }


step_size = 0.0078125


def gather_taps(stacked, row_len):
    out_rows = stacked.shape[2] // row_len - 2
    out_cells = out_rows * row_len
    padded = jnp.pad(stacked, ((0, 0), (0, 0), (1, 1)))
    column = jnp.arange(out_cells, dtype=jnp.int32) % row_len
    pieces = []
    for row_off in (-1, 0, 1):
        for col_off in (-1, 0, 1):
            offset = (1 + row_off) * row_len + col_off + 1
            window = padded[:, :, offset:offset + out_cells]
            if col_off == -1:
                window = jnp.where(column != 0, window, jnp.zeros_like(window))
            elif col_off == 1:
                window = jnp.where(column != row_len - 1, window, jnp.zeros_like(window))
            pieces.append(window)
    return jnp.concatenate(pieces, axis=1)


def advance(current, kernel, bias_row, probes):
    activation = jnp.tanh(current)
    slopes = 1.0 - activation * activation
    probe_vals = probes.astype(jnp.float32)
    inputs = jnp.concatenate([activation[None], slopes[None] * probe_vals], axis=0).astype(jnp.bfloat16)
    inputs = inputs.reshape((1 + PROBES) * BATCH, CHANNELS, CELLS)
    extended = jnp.pad(inputs, ((0, 0), (0, 0), (WIDTH, WIDTH)))
    stacked = gather_taps(extended, WIDTH)
    mixing = jnp.einsum("ok,skn->son", kernel.astype(jnp.float32), stacked.astype(jnp.float32), precision=lax.Precision.HIGHEST)
    forcing = mixing[:BATCH] + bias_row[None, :, None]
    probe_out = mixing[BATCH:].reshape(PROBES, BATCH, CHANNELS, CELLS)
    trace_value = jnp.sum(probe_vals * probe_out) / (PROBES * BATCH)
    return current + step_size * forcing, trace_value


def reference(guess, kernels, biases, probes):
    group_kernels = kernels.reshape(N_TM, STEPS_DEV, CHANNELS, 9 * CHANNELS)
    group_biases = biases.reshape(N_TM, STEPS_DEV, CHANNELS)

    def run_group(bundle):
        current, layer_kernels, layer_biases = bundle
        values = []
        for layer_index in range(STEPS_DEV):
            current, trace_value = advance(current, layer_kernels[layer_index], layer_biases[layer_index], probes)
            values.append(trace_value)
        return current, jnp.stack(values)

    finals, traces = lax.map(run_group, (guess, group_kernels, group_biases))
    summed = group_kernels.astype(jnp.float32).reshape(N_TM, STEPS_DEV, CHANNELS, 9, CHANNELS).sum(axis=(1, 3))
    coarse = jnp.eye(CHANNELS, dtype=jnp.float32)[None] + step_size * summed
    offsets = finals - jnp.einsum("kij,kbjn->kbin", coarse, guess, precision=lax.Precision.HIGHEST)

    def relay_step(carried, bundle):
        matrix, offset = bundle
        advanced = jnp.einsum("ij,bjn->bin", matrix, carried, precision=lax.Precision.HIGHEST) + offset
        return advanced, advanced

    final_state, remaining = lax.scan(relay_step, finals[0], (coarse[1:N_TM - 1], offsets[1:N_TM - 1]))
    states = jnp.concatenate([guess[0:1], finals[0:1], remaining], axis=0)
    log_change = -(step_size / WIDTH) * jnp.cumsum(traces.reshape(-1))
    return states, log_change
```

```python
import functools

import jax
import jax.numpy as jnp
from jax import lax
from jax.experimental import pallas as pl
from jax.experimental.pallas import tpu as pltpu
from jax.sharding import Mesh
from jax.sharding import PartitionSpec as P

WIDTH = 64
STEP = 0.0078125
TM = ("x", "zh", "zl", "c")
NEAR = ("zl", "c")
F32 = jnp.float32
BF16 = jnp.bfloat16


def split3(m):
    hi = m.astype(BF16)
    return hi, (m - hi.astype(F32)).astype(BF16)


def left3(m):
    hi, lo = split3(m)
    return jnp.concatenate([hi, hi, lo], axis=1)


def right3(v):
    hi, lo = split3(v)
    return jnp.concatenate([hi, lo, hi], axis=0)


def mix(m, v):
    return jnp.dot(left3(m), right3(v), preferred_element_type=F32)


def fold(m):
    half = m.shape[0] // 2
    return jnp.concatenate([m[:half], m[half:]], axis=1)


def unfold(m):
    half = m.shape[1] // 2
    return jnp.concatenate([m[:, :half], m[:, half:]], axis=0)


def eye(n):
    return (
        lax.broadcasted_iota(jnp.int32, (n, n), 0) == lax.broadcasted_iota(jnp.int32, (n, n), 1)
    ).astype(F32)


def edge_kernel(g_first, g_last, p_first, p_last, up_ref, down_ref):
    up_ref[:64] = g_first[0, 0]
    down_ref[:64] = g_last[0, 0]
    first = [p_first[n, 0].astype(F32)[:, :WIDTH] for n in range(2)]
    last = [p_last[n, 0].astype(F32)[:, WIDTH:] for n in range(2)]
    up_ref[64:] = jnp.concatenate(first, axis=1)
    down_ref[64:] = jnp.concatenate(last, axis=1)


def edges(guess, probes):
    last = guess.shape[3] // 128 - 1
    g_block, p_block = (1, 1, 64, 128), (2, 1, 64, 128)
    return pl.pallas_call(
        edge_kernel,
        grid=(1,),
        in_specs=[
            pl.BlockSpec(g_block, lambda i: (0, 0, 0, 0)),
            pl.BlockSpec(g_block, lambda i: (0, 0, 0, last)),
            pl.BlockSpec(p_block, lambda i: (0, 0, 0, 0)),
            pl.BlockSpec(p_block, lambda i: (0, 0, 0, last)),
        ],
        out_specs=[pl.BlockSpec((128, 128), lambda i: (0, 0))] * 2,
        out_shape=[jax.ShapeDtypeStruct((128, 128), F32)] * 2,
        name="edges",
    )(guess, guess, probes, probes)


def taps(v, column):
    n = v.shape[1]
    left = pltpu.roll(jnp.where(column == WIDTH - 1, 0.0, v), 1, 1)
    right = pltpu.roll(jnp.where(column == 0, 0.0, v), n - 1, 1)
    rows = []
    for part in (left, v, right):
        above = pltpu.roll(part, WIDTH, 1)
        below = jnp.concatenate([above[:, 128:], above[:, :128]], axis=1)
        rows.append((above, part, below))
    return jnp.concatenate(
        [rows[dx][dy].astype(BF16) for dy in range(3) for dx in range(3)], axis=0
    )


def steps_kernel(place_ref, g_ref, low_ref, high_ref, p_ref, k_ref, b_ref, send_ref, t_ref):
    strip_first, strip_last, leading = place_ref[0] == 1, place_ref[1] == 1, place_ref[2] == 1
    g = g_ref[0, 0]
    cells = g.shape[1]
    wide = cells + 256
    lane = lax.broadcasted_iota(jnp.int32, (64, wide), 1)
    column = lane & (WIDTH - 1)
    outside = (strip_first & (lane < 128)) | (strip_last & (lane >= wide - 128))
    zero = jnp.zeros((64, WIDTH), F32)
    probe_mid = [p_ref[n, 0].astype(F32) for n in range(2)]
    probe = [
        jnp.concatenate(
            [
                zero,
                low_ref[64:, n * WIDTH : (n + 1) * WIDTH],
                probe_mid[n],
                high_ref[64:, n * WIDTH : (n + 1) * WIDTH],
                zero,
            ],
            axis=1,
        )
        for n in range(2)
    ]
    diagonal = eye(64) == 1.0
    current = jnp.concatenate([low_ref[:64], g, high_ref[:64]], axis=1)
    moved = jnp.zeros((64, cells), F32)
    rows = lax.broadcasted_iota(jnp.int32, (8, 128), 0)
    trace = jnp.zeros((8, 128), F32)
    for layer in range(2):
        kernel = k_ref[layer]
        bias = jnp.sum(
            jnp.where(diagonal, b_ref[layer : layer + 1, :], 0.0), axis=1, keepdims=True
        )
        activation = jnp.tanh(current)
        if layer:
            activation = jnp.where(outside, 0.0, activation)
        slopes = 1.0 - activation * activation
        stack = taps(activation.astype(BF16).astype(F32), column)
        if layer:
            stack = stack[:, 128 : 128 + cells]
        forcing = jnp.dot(kernel, stack, preferred_element_type=F32) + bias
        total = jnp.zeros((64, cells), F32)
        for n in range(2):
            stack = taps((slopes * probe[n]).astype(BF16).astype(F32), column)
            inner = jnp.dot(kernel, stack[:, 128 : 128 + cells], preferred_element_type=F32)
            total = total + probe_mid[n] * inner
        trace = jnp.where(rows == layer, 0.5 * jnp.sum(total), trace)
        if layer:
            moved = moved + STEP * forcing
        else:
            current = current + STEP * forcing
            moved = moved + STEP * forcing[:, 128 : 128 + cells]
    t_ref[...] = trace
    both = k_ref[0].astype(F32) + k_ref[1].astype(F32)
    pair = both[:, :128] + both[:, 128:256] + both[:, 256:384] + both[:, 384:512]
    coarse = STEP * (pair[:, :64] + pair[:, 64:] + both[:, 512:])
    offset = jnp.where(leading, moved + g, moved - mix(coarse, g))
    change = fold(jnp.where(leading, -eye(64), coarse))
    for j in range(cells // 128):
        send_ref[j, :64] = offset[:, j * 128 : (j + 1) * 128]
        send_ref[j, 64:] = change


def whole(*shape):
    return pl.BlockSpec(memory_space=pltpu.VMEM)


def scalars():
    return pl.BlockSpec(memory_space=pltpu.SMEM)


def call(kernel, shapes, places, args, name):
    return pl.pallas_call(
        kernel,
        in_specs=[scalars()] * places + [whole()] * (len(args) - places),
        out_specs=[whole()] * len(shapes),
        out_shape=[jax.ShapeDtypeStruct(s, F32) for s in shapes],
        name=name,
    )(*args)


def advance(matrix, value, change, offset):
    wide = jnp.concatenate([value, matrix], axis=1)
    moved = wide + mix(change, wide)
    return moved[:, 128:], moved[:, :128] + offset


def near_kernel(r_ref, t_ref, send_ref, value_ref, matrix_ref):
    count = r_ref.shape[0]
    matrix, value = eye(64), jnp.zeros((64, 128), F32)
    for j in range(count):
        value_ref[j] = value
        matrix_ref[j] = matrix
        matrix, value = advance(matrix, value, unfold(r_ref[j, 64:96]), r_ref[j, :64])
    change = fold(matrix - eye(64))
    for i in range(send_ref.shape[0]):
        send_ref[i, :64] = value
        send_ref[i, 64:96] = change
        send_ref[i, 96:] = t_ref[...]


def far_kernel(place_ref, r_ref, send_ref, value_ref, matrix_ref, t_ref):
    count = r_ref.shape[0]
    me = place_ref[0]
    rows = lax.broadcasted_iota(jnp.int32, (8, 128), 0)
    matrix, value = eye(64), jnp.zeros((64, 128), F32)
    own_matrix, own_value = matrix, value
    before = total = own = jnp.zeros((8, 128), F32)
    for i in range(count):
        own_matrix = jnp.where(me == i, matrix, own_matrix)
        own_value = jnp.where(me == i, value, own_value)
        t = r_ref[i, 96:]
        before = jnp.where(me == i, total, before)
        own = jnp.where(me == i, t, own)
        total = total + t
        matrix, value = advance(matrix, value, unfold(r_ref[i, 64:96]), r_ref[i, :64])
    value_ref[...] = own_value
    matrix_ref[...] = own_matrix
    spread = jnp.sum(before, axis=0, keepdims=True)
    t_ref[...] = jnp.where(rows == 2, spread, own)
    change = fold(matrix - eye(64))
    for i in range(send_ref.shape[0]):
        send_ref[i, :64] = value
        send_ref[i, 64:96] = change
        send_ref[i, 96:] = total


def back_kernel(place_ref, r_ref, far_value, far_matrix, t_ref, near_value, near_matrix, send_ref):
    me = place_ref[0]
    rows = lax.broadcasted_iota(jnp.int32, (8, 128), 0)
    state = own = jnp.zeros((64, 128), F32)
    before = total = jnp.zeros((8, 128), F32)
    count = r_ref.shape[0]
    for i in range(count):
        own = jnp.where(me == i, state, own)
        before = jnp.where(me == i, total, before)
        total = total + r_ref[i, 96:]
        if i < count - 1:
            state = state + mix(unfold(r_ref[i, 64:96]), state) + r_ref[i, :64]
    entry = mix(far_matrix[...], own) + far_value[...]
    near = near_matrix.shape[0]
    states = mix(near_matrix[...].reshape(near * 64, 64), entry)
    spread = jnp.sum(before, axis=0, keepdims=True)
    t = t_ref[...] + jnp.where(rows == 2, spread, 0.0)
    for j in range(near):
        send_ref[j, :64] = states[j * 64 : (j + 1) * 64] + near_value[j]
        send_ref[j, 64:] = t


def final_kernel(place_ref, r_ref, g_ref, state_ref, log_ref):
    leading, me = place_ref[0] == 1, place_ref[1]
    count = r_ref.shape[0]
    rows = lax.broadcasted_iota(jnp.int32, (8, 128), 0)
    earlier = jnp.zeros((1, 128), F32)
    own = jnp.zeros((8, 128), F32)
    for j in range(count):
        at = slice(j * 128, (j + 1) * 128)
        state_ref[0, 0, :, at] = jnp.where(leading, g_ref[0, 0, :, at], r_ref[j, :64])
        t = r_ref[j, 64:]
        earlier = earlier + t[2:3] + jnp.where(j < me, t[0:1] + t[1:2], 0.0)
        own = jnp.where(me == j, t, own)
    first = earlier + own[0:1]
    second = first + own[1:2]
    log_ref[...] = -(STEP / WIDTH) * jnp.where(rows == 0, first, second)


def body(guess, kernels, biases, probes):
    strips = lax.axis_size("space")
    strip = lax.axis_index("space")
    near = lax.axis_size("zl") * lax.axis_size("c")
    far, last = lax.axis_size("zh"), lax.axis_size("x")
    leading = (lax.axis_index(TM) == 0).astype(jnp.int32)
    cells = guess.shape[3]

    up, down = edges(guess, probes)
    forward = [(i, i + 1) for i in range(strips - 1)]
    backward = [(i + 1, i) for i in range(strips - 1)]
    low = lax.ppermute(down, "space", forward)
    high = lax.ppermute(up, "space", backward)

    place = jnp.stack(
        [(strip == 0).astype(jnp.int32), (strip == strips - 1).astype(jnp.int32), leading]
    )
    send, trace = call(
        steps_kernel,
        [(near, 96, 128), (8, 128)],
        1,
        (place, guess, low, high, probes, kernels, biases),
        "steps",
    )
    hop = 1
    while hop < strips:
        trace = trace + lax.ppermute(trace, "space", [(i, i ^ hop) for i in range(strips)])
        hop *= 2
    got = lax.all_to_all(send, NEAR, 0, 0, tiled=True)
    send, near_value, near_matrix = call(
        near_kernel,
        [(far, 104, 128), (near, 64, 128), (near, 64, 64)],
        0,
        (got, trace),
        "near",
    )
    got = lax.all_to_all(send, "zh", 0, 0, tiled=True)
    send, far_value, far_matrix, trace = call(
        far_kernel,
        [(last, 104, 128), (64, 128), (64, 64), (8, 128)],
        1,
        (lax.axis_index("zh").reshape(1), got),
        "far",
    )
    got = lax.all_to_all(send, "x", 0, 0, tiled=True)
    (send,) = call(
        back_kernel,
        [(near, 72, 128)],
        1,
        (lax.axis_index("x").reshape(1), got, far_value, far_matrix, trace, near_value, near_matrix),
        "back",
    )
    got = lax.all_to_all(send, NEAR, 0, 0, tiled=True)
    place = jnp.stack([leading, lax.axis_index(NEAR)])
    states, log_change = call(
        final_kernel, [(1, 1, 64, cells), (8, 128)], 1, (place, got, guess), "final"
    )
    return states, log_change[:2, 0]


def solution(mesh):
    finer = Mesh(
        mesh.devices.reshape(4, 4, 4, 2, mesh.shape["space"]), ("x", "zh", "zl", "c", "space")
    )
    placed = (
        P(TM, None, None, "space"),
        P(TM, None, None),
        P(TM, None),
        P(None, None, None, "space"),
    )
    return jax.shard_map(
        body,
        mesh=finer,
        in_specs=placed,
        out_specs=(P(TM, None, None, "space"), P(TM)),
        check_vma=False,
    )
```

```python
import functools

import jax
import jax.numpy as jnp
from jax import lax
from jax.experimental import pallas as pl
from jax.experimental.pallas import tpu as pltpu
from jax.sharding import Mesh
from jax.sharding import PartitionSpec as P

WIDTH = 64
STEP = 0.0078125
TM = ("x", "zh", "zl", "c")
NEAR = ("zl", "c")
F32 = jnp.float32
BF16 = jnp.bfloat16


def split3(m):
    hi = m.astype(BF16)
    return hi, (m - hi.astype(F32)).astype(BF16)


def left3(m):
    hi, lo = split3(m)
    return jnp.concatenate([hi, hi, lo], axis=1)


def right3(v):
    hi, lo = split3(v)
    return jnp.concatenate([hi, lo, hi], axis=0)


def mix(m, v):
    return jnp.dot(left3(m), right3(v), preferred_element_type=F32)


def fold(m):
    half = m.shape[0] // 2
    return jnp.concatenate([m[:half], m[half:]], axis=1)


def unfold(m):
    half = m.shape[1] // 2
    return jnp.concatenate([m[:, :half], m[:, half:]], axis=0)


def eye(n):
    return (
        lax.broadcasted_iota(jnp.int32, (n, n), 0) == lax.broadcasted_iota(jnp.int32, (n, n), 1)
    ).astype(F32)


def edge_kernel(g_ref, p_ref, up_ref, down_ref, p_first, p_last, sems):
    end = g_ref.shape[3] - 128
    copies = [
        pltpu.make_async_copy(p_ref.at[:, 0, :, pl.ds(0, 128)], p_first, sems.at[0]),
        pltpu.make_async_copy(p_ref.at[:, 0, :, pl.ds(end, 128)], p_last, sems.at[1]),
        pltpu.make_async_copy(g_ref.at[0, 0, :, pl.ds(0, 128)], up_ref.at[pl.ds(0, 64)], sems.at[2]),
        pltpu.make_async_copy(
            g_ref.at[0, 0, :, pl.ds(end, 128)], down_ref.at[pl.ds(0, 64)], sems.at[3]
        ),
    ]
    for copy in copies:
        copy.start()
    for copy in copies[:2]:
        copy.wait()
    up_ref[64:] = jnp.concatenate([p_first[n].astype(F32)[:, :WIDTH] for n in range(2)], axis=1)
    down_ref[64:] = jnp.concatenate([p_last[n].astype(F32)[:, WIDTH:] for n in range(2)], axis=1)
    for copy in copies[2:]:
        copy.wait()


def edges(guess, probes):
    return pl.pallas_call(
        edge_kernel,
        in_specs=[pl.BlockSpec(memory_space=pltpu.HBM)] * 2,
        out_specs=[whole()] * 2,
        out_shape=[jax.ShapeDtypeStruct((128, 128), F32)] * 2,
        scratch_shapes=[pltpu.VMEM((2, 64, 128), BF16)] * 2 + [pltpu.SemaphoreType.DMA((4,))],
        compiler_params=pltpu.CompilerParams(vmem_limit_bytes=(64 << 20) - (256 << 10)),
        name="edges",
    )(guess, probes)


def taps(v):
    n = v.shape[1]
    column = lax.broadcasted_iota(jnp.int32, v.shape, 1) & (WIDTH - 1)
    left = pltpu.roll(jnp.where(column == WIDTH - 1, 0.0, v), 1, 1)
    right = pltpu.roll(jnp.where(column == 0, 0.0, v), n - 1, 1)
    rows = []
    for part in (left, v, right):
        above = pltpu.roll(part, WIDTH, 1)
        below = jnp.concatenate([above[:, 128:], above[:, :128]], axis=1)
        rows.append((above, part, below))
    return jnp.concatenate(
        [rows[dx][dy].astype(BF16) for dy in range(3) for dx in range(3)], axis=0
    )


def rounded(v):
    return v.astype(BF16).astype(F32)


def convolve(kernel, v, at=None):
    stack = taps(rounded(v))
    return jnp.dot(kernel, stack if at is None else stack[:, at], preferred_element_type=F32)


def bias_of(b_ref, layer):
    return jnp.sum(
        jnp.where(eye(64) == 1.0, b_ref[layer : layer + 1, :], 0.0), axis=1, keepdims=True
    )


def side(ref, n):
    return ref[64:, n * WIDTH : (n + 1) * WIDTH]


def inner_kernel(place_ref, g_ref, p_ref, k_ref, b_ref, state_ref, offset_ref, change_ref, t_ref):
    leading = place_ref[0] == 0
    g = g_ref[0, 0]
    cells = g.shape[1]
    kernel = k_ref[0]
    activation = jnp.tanh(g)
    slopes = 1.0 - activation * activation
    forcing = STEP * (convolve(kernel, activation) + bias_of(b_ref, 0))
    total = jnp.zeros((64, cells), F32)
    for n in range(2):
        probe = p_ref[n, 0].astype(F32)
        total = total + probe * convolve(kernel, slopes * probe)
    lane = lax.broadcasted_iota(jnp.int32, (64, cells), 1)
    total = jnp.where((lane >= WIDTH) & (lane < cells - WIDTH), total, 0.0)
    t_ref[...] = jnp.full((8, 128), 0.5 * jnp.sum(total))
    both = k_ref[0].astype(F32) + k_ref[1].astype(F32)
    pair = both[:, :128] + both[:, 128:256] + both[:, 256:384] + both[:, 384:512]
    coarse = STEP * (pair[:, :64] + pair[:, 64:] + both[:, 512:])
    state_ref[...] = g + forcing
    offset_ref[...] = forcing + jnp.where(leading, g, -mix(coarse, g))
    change_ref[...] = fold(jnp.where(leading, -eye(64), coarse))


def outer_kernel(
    strips,
    strip_ref,
    g_ref,
    low_ref,
    high_ref,
    p_ref,
    k_ref,
    b_ref,
    state_ref,
    offset_ref,
    change_ref,
    inner_ref,
    send_ref,
    t_ref,
):
    cells = state_ref.shape[1]
    last = cells - 128
    zero = jnp.zeros((64, WIDTH), F32)
    ends = jnp.concatenate(
        [low_ref[:64], g_ref[0, 0, :, :128], g_ref[0, 0, :, last:], high_ref[:64]], axis=1
    )
    probe_mid = [p_ref[n, 0].astype(F32) for n in range(2)]
    activation = jnp.tanh(ends)
    slopes = 1.0 - activation * activation
    kernel = k_ref[0]
    forcing = STEP * (convolve(kernel, activation) + bias_of(b_ref, 0))
    total = jnp.zeros((64, 128), F32)
    for n in range(2):
        probe = jnp.concatenate(
            [
                zero,
                side(low_ref, n),
                probe_mid[n][:, :128],
                probe_mid[n][:, last:],
                side(high_ref, n),
                zero,
            ],
            axis=1,
        )
        found = convolve(kernel, slopes * probe, slice(128, 384))
        total = total + jnp.concatenate(
            [
                probe_mid[n][:, :WIDTH] * found[:, :WIDTH],
                probe_mid[n][:, last + WIDTH :] * found[:, 256 - WIDTH :],
            ],
            axis=1,
        )
    rows = lax.broadcasted_iota(jnp.int32, (8, 128), 0)
    trace = inner_ref[...] + 0.5 * jnp.sum(total)

    lane = lax.broadcasted_iota(jnp.int32, (64, 128), 1)
    fresh = ends + forcing
    first, final = state_ref[:, :128], state_ref[:, last:]
    new_first = jnp.where(lane < WIDTH, fresh[:, 128:256], first)
    new_final = jnp.where(lane < WIDTH, final, fresh[:, 256:384])
    current = jnp.concatenate(
        [fresh[:, :128], new_first, state_ref[:, 128:last], new_final, fresh[:, 384:]], axis=1
    )
    wide = cells + 256
    far_lane = lax.broadcasted_iota(jnp.int32, (64, wide), 1)
    outside = ((strip_ref[0] == 0) & (far_lane < 128)) | (
        (strip_ref[0] == strips - 1) & (far_lane >= wide - 128)
    )
    middle = slice(128, 128 + cells)
    activation = jnp.where(outside, 0.0, jnp.tanh(current))
    slopes = 1.0 - activation * activation
    kernel = k_ref[1]
    forcing = STEP * (convolve(kernel, activation, middle) + bias_of(b_ref, 1))
    total = jnp.zeros((64, cells), F32)
    for n in range(2):
        probe = jnp.concatenate(
            [zero, side(low_ref, n), probe_mid[n], side(high_ref, n), zero], axis=1
        )
        total = total + probe_mid[n] * convolve(kernel, slopes * probe, middle)
    trace = jnp.where(rows == 1, 0.5 * jnp.sum(total), jnp.where(rows == 0, trace, 0.0))
    t_ref[...] = trace
    for j in range(cells // 128):
        at = slice(j * 128, (j + 1) * 128)
        part = offset_ref[:, at] + forcing[:, at]
        if j == 0:
            part = part + (new_first - first)
        if j == cells // 128 - 1:
            part = part + (new_final - final)
        send_ref[j, :64] = part
        send_ref[j, 64:] = change_ref[...]


def whole(*shape):
    return pl.BlockSpec(memory_space=pltpu.VMEM)


def scalars():
    return pl.BlockSpec(memory_space=pltpu.SMEM)


def call(kernel, shapes, places, args, name, room, cost=None):
    return pl.pallas_call(
        kernel,
        in_specs=[scalars()] * places + [whole()] * (len(args) - places),
        out_specs=[whole() if len(s) > 1 else scalars() for s in shapes],
        out_shape=[jax.ShapeDtypeStruct(s, F32) for s in shapes],
        compiler_params=pltpu.CompilerParams(vmem_limit_bytes=room << 20),
        cost_estimate=cost,
        name=name,
    )(*args)


def advance(matrix, value, change, offset):
    wide = jnp.concatenate([value, matrix], axis=1)
    moved = wide + mix(change, wide)
    return moved[:, 128:], moved[:, :128] + offset


def join(earlier, later):
    change, offset = later
    wide = jnp.concatenate([earlier[1], earlier[0]], axis=1)
    moved = wide + mix(change, wide)
    return moved[:, 128:] + change, moved[:, :128] + offset


def near_kernel(r_ref, *refs):
    traces, (send_ref, value_ref, matrix_ref) = refs[:-3], refs[-3:]
    count = r_ref.shape[0]
    spans = [(unfold(r_ref[j, 64:96]), r_ref[j, :64]) for j in range(count)]
    before = [None] + spans[:1]
    pairs = [join(spans[j], spans[j + 1]) for j in range(0, count, 2)]
    upto = pairs[:1]
    if count == 8:
        quads = [join(pairs[0], pairs[1]), join(pairs[2], pairs[3])]
        total = join(quads[0], quads[1])
        upto = [pairs[0], quads[0], join(quads[0], pairs[2])]
    else:
        total = join(pairs[0], pairs[1])
    for i, span in enumerate(upto):
        before += [span, join(span, spans[2 * i + 2])]
    for j in range(count):
        matrix, value = before[j] if j else (jnp.zeros((64, 64), F32), jnp.zeros((64, 128), F32))
        value_ref[j] = value
        matrix_ref[j] = matrix
    change, value = fold(total[0]), total[1]
    trace = sum(t[...] for t in traces)
    for i in range(send_ref.shape[0]):
        send_ref[i, :64] = value
        send_ref[i, 64:96] = change
        send_ref[i, 96:] = trace


def far_kernel(place_ref, r_ref, send_ref, value_ref, matrix_ref, t_ref):
    count = r_ref.shape[0]
    me = place_ref[0]
    rows = lax.broadcasted_iota(jnp.int32, (8, 128), 0)
    matrix, value = eye(64), jnp.zeros((64, 128), F32)
    own_matrix, own_value = matrix, value
    before = total = own = jnp.zeros((8, 128), F32)
    for i in range(count):
        own_matrix = jnp.where(me == i, matrix, own_matrix)
        own_value = jnp.where(me == i, value, own_value)
        t = r_ref[i, 96:]
        before = jnp.where(me == i, total, before)
        own = jnp.where(me == i, t, own)
        total = total + t
        matrix, value = advance(matrix, value, unfold(r_ref[i, 64:96]), r_ref[i, :64])
    value_ref[...] = own_value
    matrix_ref[...] = own_matrix
    spread = jnp.sum(before, axis=0, keepdims=True)
    t_ref[...] = jnp.where(rows == 2, spread, own)
    change = fold(matrix - eye(64))
    for i in range(send_ref.shape[0]):
        send_ref[i, :64] = value
        send_ref[i, 64:96] = change
        send_ref[i, 96:] = total


def back_kernel(place_ref, r_ref, far_value, far_matrix, t_ref, near_value, near_matrix, send_ref):
    me = place_ref[0]
    rows = lax.broadcasted_iota(jnp.int32, (8, 128), 0)
    state = own = jnp.zeros((64, 128), F32)
    before = total = jnp.zeros((8, 128), F32)
    count = r_ref.shape[0]
    for i in range(count):
        own = jnp.where(me == i, state, own)
        before = jnp.where(me == i, total, before)
        total = total + r_ref[i, 96:]
        if i < count - 1:
            state = state + mix(unfold(r_ref[i, 64:96]), state) + r_ref[i, :64]
    entry = mix(far_matrix[...], own) + far_value[...]
    near = near_matrix.shape[0]
    states = mix(near_matrix[...].reshape(near * 64, 64), entry)
    spread = jnp.sum(before, axis=0, keepdims=True)
    t = t_ref[...] + jnp.where(rows == 2, spread, 0.0)
    for j in range(near):
        send_ref[j, :64] = entry + states[j * 64 : (j + 1) * 64] + near_value[j]
        send_ref[j, 64:] = t


def final_kernel(place_ref, me_ref, r_ref, g_ref, state_ref, log_ref):
    leading, me = place_ref[0] == 0, me_ref[0]
    count = r_ref.shape[0]
    earlier = jnp.zeros((1, 128), F32)
    own = jnp.zeros((8, 128), F32)
    for j in range(count):
        at = slice(j * 128, (j + 1) * 128)
        state_ref[0, 0, :, at] = jnp.where(leading, g_ref[0, 0, :, at], r_ref[j, :64])
        t = r_ref[j, 64:]
        earlier = earlier + t[2:3] + jnp.where(j < me, t[0:1] + t[1:2], 0.0)
        own = jnp.where(me == j, t, own)
    first = earlier + own[0:1]
    second = first + own[1:2]
    log_ref[0] = -(STEP / WIDTH) * first[0, 0]
    log_ref[1] = -(STEP / WIDTH) * second[0, 0]


def body(guess, kernels, biases, probes):
    strips = lax.axis_size("space")
    strip = lax.axis_index("space")
    near = lax.axis_size("zl") * lax.axis_size("c")
    far, last = lax.axis_size("zh"), lax.axis_size("x")
    cells = guess.shape[3]
    place = lax.axis_index(TM).reshape(1)

    up, down = edges(guess, probes)
    forward = [(i, i + 1) for i in range(strips - 1)]
    backward = [(i + 1, i) for i in range(strips - 1)]
    low = lax.ppermute(down, "space", forward)
    high = lax.ppermute(up, "space", backward)
    state, offset, change, inner = call(
        inner_kernel,
        [(64, cells), (64, cells), (32, 128), (8, 128)],
        1,
        (place, guess, probes, kernels, biases),
        "inner",
        20,
        pl.CostEstimate(flops=450_000_000, bytes_accessed=2_000_000, transcendentals=65536),
    )
    send, trace = call(
        functools.partial(outer_kernel, strips),
        [(near, 96, 128), (8, 128)],
        1,
        (
            strip.reshape(1), guess, low, high, probes, kernels, biases,
            state, offset, change, inner,
        ),
        "outer",
        20,
    )
    got = lax.all_to_all(send, NEAR, 0, 0, tiled=True)
    traces = [
        lax.ppermute(trace, "space", [(i, (i + hop) % strips) for i in range(strips)])
        for hop in range(1, strips)
    ]
    send, near_value, near_matrix = call(
        near_kernel,
        [(far, 104, 128), (near, 64, 128), (near, 64, 64)],
        0,
        (got, trace, *traces),
        "near",
        8,
    )
    got = lax.all_to_all(send, "zh", 0, 0, tiled=True)
    send, far_value, far_matrix, trace = call(
        far_kernel,
        [(last, 104, 128), (64, 128), (64, 64), (8, 128)],
        1,
        (lax.axis_index("zh").reshape(1), got),
        "far",
        8,
    )
    got = lax.all_to_all(send, "x", 0, 0, tiled=True)
    (send,) = call(
        back_kernel,
        [(near, 72, 128)],
        1,
        (lax.axis_index("x").reshape(1), got, far_value, far_matrix, trace, near_value, near_matrix),
        "back",
        8,
    )
    got = lax.all_to_all(send, NEAR, 0, 0, tiled=True)
    return call(
        final_kernel,
        [(1, 1, 64, cells), (2,)],
        2,
        (place, lax.axis_index(NEAR).reshape(1), got, guess),
        "final",
        8,
    )


def solution(mesh):
    finer = Mesh(
        mesh.devices.reshape(4, 4, 4, 2, mesh.shape["space"]), ("x", "zh", "zl", "c", "space")
    )
    placed = (
        P(TM, None, None, "space"),
        P(TM, None, None),
        P(TM, None),
        P(None, None, None, "space"),
    )
    return jax.shard_map(
        body,
        mesh=finer,
        in_specs=placed,
        out_specs=(P(TM, None, None, "space"), P(TM)),
        check_vma=False,
    )
```

```python
import functools

import jax
import jax.numpy as jnp
from jax import lax
from jax.experimental import pallas as pl
from jax.experimental.pallas import tpu as pltpu
from jax.sharding import Mesh
from jax.sharding import PartitionSpec as P

WIDTH = 64
STEP = 0.0078125
TM = ("x", "zh", "zl", "c")
NEAR = ("zl", "c")
SPACE = ("sh", "sl")
VALUE_SCALE = 2048.0
CHANGE_SCALE = 32768.0
F16 = jnp.float16
F32 = jnp.float32
BF16 = jnp.bfloat16


def split3(m):
    hi = m.astype(BF16)
    return hi, (m - hi.astype(F32)).astype(BF16)


def left3(m):
    hi, lo = split3(m)
    return jnp.concatenate([hi, hi, lo], axis=1)


def right3(v):
    hi, lo = split3(v)
    return jnp.concatenate([hi, lo, hi], axis=0)


def mix(m, v):
    return jnp.dot(left3(m), right3(v), preferred_element_type=F32)


def fold(m):
    half = m.shape[0] // 2
    return jnp.concatenate([m[:half], m[half:]], axis=1)


def unfold(m):
    half = m.shape[1] // 2
    return jnp.concatenate([m[:, :half], m[:, half:]], axis=0)


def eye(n):
    return (
        lax.broadcasted_iota(jnp.int32, (n, n), 0) == lax.broadcasted_iota(jnp.int32, (n, n), 1)
    ).astype(F32)


def edge_kernel(g_ref, p_ref, up_ref, down_ref, gv_ref, pv_ref, sems):
    end = g_ref.shape[3] - 128
    copies = [
        pltpu.make_async_copy(p_ref, pv_ref, sems.at[0]),
        pltpu.make_async_copy(g_ref, gv_ref, sems.at[1]),
    ]
    for copy in copies:
        copy.start()
    copies[0].wait()
    first = [pv_ref[n, 0, :, :WIDTH].astype(F32) for n in range(2)]
    last = [pv_ref[n, 0, :, end + WIDTH :].astype(F32) for n in range(2)]
    up_ref[64:] = jnp.concatenate(first, axis=1)
    down_ref[64:] = jnp.concatenate(last, axis=1)
    copies[1].wait()
    up_ref[:64] = gv_ref[0, 0, :, :128]
    down_ref[:64] = gv_ref[0, 0, :, end:]


def edges(guess, probes):
    held = [pltpu.with_memory_space_constraint(v, pltpu.HBM) for v in (guess, probes)]
    return pl.pallas_call(
        edge_kernel,
        in_specs=[pl.BlockSpec(memory_space=pltpu.HBM)] * 2,
        out_specs=[whole()] * 4,
        out_shape=[jax.ShapeDtypeStruct((128, 128), F32)] * 2
        + [jax.ShapeDtypeStruct(guess.shape, F32), jax.ShapeDtypeStruct(probes.shape, BF16)],
        scratch_shapes=[pltpu.SemaphoreType.DMA((2,))],
        compiler_params=pltpu.CompilerParams(vmem_limit_bytes=4 << 20),
        name="edges",
    )(*held)


def taps(v):
    n = v.shape[1]
    column = lax.broadcasted_iota(jnp.int32, v.shape, 1) & (WIDTH - 1)
    left = pltpu.roll(jnp.where(column == WIDTH - 1, 0.0, v), 1, 1)
    right = pltpu.roll(jnp.where(column == 0, 0.0, v), n - 1, 1)
    rows = []
    for part in (left, v, right):
        above = pltpu.roll(part, WIDTH, 1)
        below = jnp.concatenate([above[:, 128:], above[:, :128]], axis=1)
        rows.append((above, part, below))
    return jnp.concatenate(
        [rows[dx][dy].astype(BF16) for dy in range(3) for dx in range(3)], axis=0
    )


def rounded(v):
    return v.astype(BF16).astype(F32)


def convolve(kernel, v, at=None):
    stack = taps(rounded(v))
    return jnp.dot(kernel, stack if at is None else stack[:, at], preferred_element_type=F32)


def bias_of(b_ref, layer):
    return jnp.sum(
        jnp.where(eye(64) == 1.0, b_ref[layer : layer + 1, :], 0.0), axis=1, keepdims=True
    )


def side(ref, n):
    return ref[64:, n * WIDTH : (n + 1) * WIDTH]


def inner_kernel(place_ref, g_ref, p_ref, k_ref, b_ref, state_ref, offset_ref, change_ref, t_ref):
    leading = place_ref[0] == 0
    g = g_ref[0, 0]
    cells = g.shape[1]
    kernel = k_ref[0]
    activation = jnp.tanh(g)
    slopes = 1.0 - activation * activation
    forcing = STEP * (convolve(kernel, activation) + bias_of(b_ref, 0))
    total = jnp.zeros((64, cells), F32)
    for n in range(2):
        probe = p_ref[n, 0].astype(F32)
        total = total + probe * convolve(kernel, slopes * probe)
    lane = lax.broadcasted_iota(jnp.int32, (64, cells), 1)
    total = jnp.where((lane >= WIDTH) & (lane < cells - WIDTH), total, 0.0)
    t_ref[...] = jnp.full((8, 128), 0.5 * jnp.sum(total))
    both = k_ref[0].astype(F32) + k_ref[1].astype(F32)
    pair = both[:, :128] + both[:, 128:256] + both[:, 256:384] + both[:, 384:512]
    coarse = STEP * (pair[:, :64] + pair[:, 64:] + both[:, 512:])
    state_ref[...] = g + forcing
    offset_ref[...] = forcing + jnp.where(leading, g, -mix(coarse, g))
    change_ref[...] = fold(jnp.where(leading, -eye(64), coarse))


def outer_kernel(
    strips,
    strip_ref,
    g_ref,
    low_ref,
    high_ref,
    p_ref,
    k_ref,
    b_ref,
    state_ref,
    offset_ref,
    change_ref,
    inner_ref,
    send_ref,
    t_ref,
):
    cells = state_ref.shape[1]
    last = cells - 128
    zero = jnp.zeros((64, WIDTH), F32)
    ends = jnp.concatenate(
        [low_ref[:64], g_ref[0, 0, :, :128], g_ref[0, 0, :, last:], high_ref[:64]], axis=1
    )
    probe_mid = [p_ref[n, 0].astype(F32) for n in range(2)]
    activation = jnp.tanh(ends)
    slopes = 1.0 - activation * activation
    kernel = k_ref[0]
    forcing = STEP * (convolve(kernel, activation) + bias_of(b_ref, 0))
    total = jnp.zeros((64, 128), F32)
    for n in range(2):
        probe = jnp.concatenate(
            [
                zero,
                side(low_ref, n),
                probe_mid[n][:, :128],
                probe_mid[n][:, last:],
                side(high_ref, n),
                zero,
            ],
            axis=1,
        )
        found = convolve(kernel, slopes * probe, slice(128, 384))
        total = total + jnp.concatenate(
            [
                probe_mid[n][:, :WIDTH] * found[:, :WIDTH],
                probe_mid[n][:, last + WIDTH :] * found[:, 256 - WIDTH :],
            ],
            axis=1,
        )
    rows = lax.broadcasted_iota(jnp.int32, (8, 128), 0)
    trace = inner_ref[...] + 0.5 * jnp.sum(total)

    lane = lax.broadcasted_iota(jnp.int32, (64, 128), 1)
    fresh = ends + forcing
    first, final = state_ref[:, :128], state_ref[:, last:]
    new_first = jnp.where(lane < WIDTH, fresh[:, 128:256], first)
    new_final = jnp.where(lane < WIDTH, final, fresh[:, 256:384])
    current = jnp.concatenate(
        [fresh[:, :128], new_first, state_ref[:, 128:last], new_final, fresh[:, 384:]], axis=1
    )
    wide = cells + 256
    far_lane = lax.broadcasted_iota(jnp.int32, (64, wide), 1)
    outside = ((strip_ref[0] == 0) & (far_lane < 128)) | (
        (strip_ref[0] == strips - 1) & (far_lane >= wide - 128)
    )
    middle = slice(128, 128 + cells)
    activation = jnp.where(outside, 0.0, jnp.tanh(current))
    slopes = 1.0 - activation * activation
    kernel = k_ref[1]
    forcing = STEP * (convolve(kernel, activation, middle) + bias_of(b_ref, 1))
    total = jnp.zeros((64, cells), F32)
    for n in range(2):
        probe = jnp.concatenate(
            [zero, side(low_ref, n), probe_mid[n], side(high_ref, n), zero], axis=1
        )
        total = total + probe_mid[n] * convolve(kernel, slopes * probe, middle)
    trace = jnp.where(rows == 1, 0.5 * jnp.sum(total), jnp.where(rows == 0, trace, 0.0))
    t_ref[...] = trace
    for j in range(cells // 128):
        at = slice(j * 128, (j + 1) * 128)
        part = offset_ref[:, at] + forcing[:, at]
        if j == 0:
            part = part + (new_first - first)
        if j == cells // 128 - 1:
            part = part + (new_final - final)
        send_ref[j, :64] = VALUE_SCALE * part
        send_ref[j, 64:] = CHANGE_SCALE * change_ref[...]


def whole(*shape):
    return pl.BlockSpec(memory_space=pltpu.VMEM)


def scalars():
    return pl.BlockSpec(memory_space=pltpu.SMEM)


def call(kernel, shapes, places, args, name, room, cost=None):
    return pl.pallas_call(
        kernel,
        in_specs=[scalars()] * places + [whole()] * (len(args) - places),
        out_specs=[whole() if len(s) > 1 else scalars() for s in shapes],
        out_shape=[jax.ShapeDtypeStruct(s, F32) for s in shapes],
        compiler_params=pltpu.CompilerParams(vmem_limit_bytes=room << 20),
        cost_estimate=cost,
        name=name,
    )(*args)


def exponent(v):
    return jnp.ceil(jnp.log2(jnp.maximum(v, 1e-30)))


def block_exponent(v):
    return exponent(jnp.max(jnp.abs(v), axis=(0, 1), keepdims=True))


def scaled(v, power):
    return v * jnp.exp2(15.0 - power)


def restored(v, power):
    return v * jnp.exp2(power - 15.0)


def tags(t, value_power, change_power):
    lane = lax.broadcasted_iota(jnp.int32, (8, 128), 1)
    power = exponent(jnp.abs(t))
    unit = t * jnp.exp2(-power)
    coarse = rounded(unit)
    fine = 256.0 * (unit - coarse)
    top = jnp.where(lane < 64, coarse, power)
    low = jnp.where(lane < 64, fine, jnp.where(lane < 96, value_power, change_power))
    return jnp.concatenate([top, low], axis=0)


def read_tags(r):
    t = (r[:8, :1] + r[8:, :1] / 256.0) * jnp.exp2(r[:8, 64:65])
    return t, r[8:9, 64:65], r[8:9, 96:97]


def put(ref, change, value, t):
    value_power, change_power = block_exponent(value), block_exponent(change)
    value = scaled(value, value_power)
    change = scaled(fold(change), change_power)
    extra = tags(t, value_power, change_power)
    for i in range(ref.shape[0]):
        ref[i, :64] = value
        ref[i, 64:96] = change
        ref[i, 96:] = extra


def take(r):
    t, value_power, change_power = read_tags(r[96:])
    return unfold(restored(r[64:96], change_power)), restored(r[:64], value_power), t


def join(earlier, later):
    change, offset = later
    wide = jnp.concatenate([earlier[1], earlier[0]], axis=1)
    moved = wide + mix(change, wide)
    return moved[:, 128:] + change, moved[:, :128] + offset


def near_kernel(r_ref, t_ref, other_ref, send_ref, value_ref, matrix_ref):
    count = r_ref.shape[0]
    spans = [
        (unfold(r_ref[j, 64:] / CHANGE_SCALE), r_ref[j, :64] / VALUE_SCALE) for j in range(count)
    ]
    before = [None] + spans[:1]
    pairs = [join(spans[j], spans[j + 1]) for j in range(0, count, 2)]
    upto = pairs[:1]
    if count == 8:
        quads = [join(pairs[0], pairs[1]), join(pairs[2], pairs[3])]
        total = join(quads[0], quads[1])
        upto = [pairs[0], quads[0], join(quads[0], pairs[2])]
    else:
        total = join(pairs[0], pairs[1])
    for i, span in enumerate(upto):
        before += [span, join(span, spans[2 * i + 2])]
    for j in range(count):
        matrix, value = before[j] if j else (jnp.zeros((64, 64), F32), jnp.zeros((64, 128), F32))
        value_ref[j] = value
        matrix_ref[j] = matrix
    put(send_ref, *total, t_ref[...] + other_ref[...])


def far_kernel(place_ref, r_ref, send_ref, value_ref, matrix_ref):
    count = r_ref.shape[0]
    me = place_ref[0]
    span = own = (jnp.zeros((64, 64), F32), jnp.zeros((64, 128), F32))
    before = total = mine = jnp.zeros((8, 1), F32)
    for i in range(count):
        own = tuple(jnp.where(me == i, new, old) for new, old in zip(span, own))
        change, value, t = take(r_ref[i])
        before = jnp.where(me == i, total, before)
        mine = jnp.where(me == i, t, mine)
        total = total + t
        span = join(span, (change, value)) if i else (change, value)
    matrix_ref[...], value_ref[...] = own
    spread = jnp.sum(before, axis=0, keepdims=True)
    t = jnp.concatenate([total[:2], mine[:2], spread, jnp.zeros((3, 1), F32)], axis=0)
    put(send_ref, *span, jnp.broadcast_to(t, (8, 128)))


def back_kernel(
    place_ref, strip_ref, r_ref, far_value, far_matrix, near_value, near_matrix, send_ref
):
    me, strip = place_ref[0], strip_ref[0]
    state = own = jnp.zeros((64, 128), F32)
    before = total = mine = jnp.zeros((8, 1), F32)
    copies = 2
    count = r_ref.shape[0] // copies
    for i in range(count):
        own = jnp.where(me == i, state, own)
        before = jnp.where(me == i, total, before)
        t = sum(read_tags(r_ref[copies * i + n, 96:])[0] for n in range(copies))
        mine = jnp.where(me == i, t, mine)
        total = total + t
        if i < count - 1:
            change, value, _ = take(r_ref[copies * i + strip])
            state = state + mix(change, state) + value
    entry = own + mix(far_matrix[...], own) + far_value[...]
    near = near_matrix.shape[0]
    states = mix(near_matrix[...].reshape(near * 64, 64), entry)
    spread = jnp.sum(before[:2], axis=0, keepdims=True)
    t = jnp.concatenate([mine[2:5], spread, jnp.zeros((4, 1), F32)], axis=0)
    t = jnp.broadcast_to(t, (8, 128))
    for j in range(near):
        state = entry + states[j * 64 : (j + 1) * 64] + near_value[j]
        power = block_exponent(state)
        send_ref[j, :64] = scaled(state, power)
        send_ref[j, 64:] = tags(t, power, power)


def final_kernel(place_ref, me_ref, r_ref, g_ref, state_ref, log_ref):
    leading, me = place_ref[0] == 0, me_ref[0]
    count = r_ref.shape[0]
    earlier = jnp.zeros((1, 1), F32)
    own = jnp.zeros((8, 1), F32)
    for j in range(count):
        at = slice(j * 128, (j + 1) * 128)
        t, power, _ = read_tags(r_ref[j, 64:])
        state = restored(r_ref[j, :64], power)
        state_ref[0, 0, :, at] = jnp.where(leading, g_ref[0, 0, :, at], state)
        earlier = earlier + t[2:3] + t[3:4] + jnp.where(j < me, t[0:1] + t[1:2], 0.0)
        own = jnp.where(me == j, t, own)
    first = earlier + own[0:1]
    second = first + own[1:2]
    log_ref[0] = -(STEP / WIDTH) * first[0, 0]
    log_ref[1] = -(STEP / WIDTH) * second[0, 0]


def exchange(v, axes):
    return lax.all_to_all(v.astype(F16), axes, 0, 0, tiled=True).astype(F32)


def body(guess, kernels, biases, probes):
    strips = lax.axis_size(SPACE)
    strip = lax.axis_index(SPACE)
    near = lax.axis_size(NEAR)
    far, last = lax.axis_size("zh"), lax.axis_size("x")
    cells = guess.shape[3]
    place = lax.axis_index(TM).reshape(1)

    up, down, guess, probes = edges(guess, probes)
    forward = [(i, i + 1) for i in range(strips - 1)]
    backward = [(i + 1, i) for i in range(strips - 1)]
    low = lax.ppermute(down, SPACE, forward)
    high = lax.ppermute(up, SPACE, backward)
    state, offset, change, inner = call(
        inner_kernel,
        [(64, cells), (64, cells), (32, 128), (8, 128)],
        1,
        (place, guess, probes, kernels, biases),
        "inner",
        20,
        pl.CostEstimate(flops=450_000_000, bytes_accessed=2_000_000, transcendentals=65536),
    )
    send, trace = call(
        functools.partial(outer_kernel, strips),
        [(near, 96, 128), (8, 128)],
        1,
        (
            strip.reshape(1), guess, low, high, probes, kernels, biases,
            state, offset, change, inner,
        ),
        "outer",
        20,
    )
    got = exchange(send, NEAR)
    other = lax.ppermute(trace, "sl", [(0, 1), (1, 0)])
    send, near_value, near_matrix = call(
        near_kernel,
        [(far, 112, 128), (near, 64, 128), (near, 64, 64)],
        0,
        (got, trace, other),
        "near",
        8,
    )
    got = exchange(send, "zh")
    send, far_value, far_matrix = call(
        far_kernel,
        [(2 * last, 112, 128), (64, 128), (64, 64)],
        1,
        (lax.axis_index("zh").reshape(1), got),
        "far",
        8,
    )
    got = exchange(send, ("x", "sh"))
    (send,) = call(
        back_kernel,
        [(near, 80, 128)],
        2,
        (
            lax.axis_index("x").reshape(1),
            lax.axis_index("sh").reshape(1),
            got,
            far_value,
            far_matrix,
            near_value,
            near_matrix,
        ),
        "back",
        8,
    )
    got = exchange(send, NEAR)
    return call(
        final_kernel,
        [(1, 1, 64, cells), (2,)],
        2,
        (place, lax.axis_index(NEAR).reshape(1), got, guess),
        "final",
        8,
    )


def solution(mesh):
    finer = Mesh(
        mesh.devices.reshape(4, 4, 4, 2, 2, 2), ("x", "zh", "zl", "c", "sh", "sl")
    )
    placed = (
        P(TM, None, None, SPACE),
        P(TM, None, None),
        P(TM, None),
        P(None, None, None, SPACE),
    )
    return jax.shard_map(
        body,
        mesh=finer,
        in_specs=placed,
        out_specs=(P(TM, None, None, SPACE), P(TM)),
        check_vma=False,
    )
```

```python
import functools

import jax
import jax.numpy as jnp
from jax import lax
from jax.experimental import pallas as pl
from jax.experimental.pallas import tpu as pltpu
from jax.sharding import Mesh
from jax.sharding import PartitionSpec as P

WIDTH = 64
STEP = 0.0078125
TM = ("x", "zh", "zl", "c")
NEAR = ("zl", "c")
SPACE = ("sh", "sl")
VALUE_SCALE = 2048.0
CHANGE_SCALE = 32768.0
F16 = jnp.float16
F32 = jnp.float32
BF16 = jnp.bfloat16


def split3(m):
    hi = m.astype(BF16)
    return hi, (m - hi.astype(F32)).astype(BF16)


def left3(m):
    hi, lo = split3(m)
    return jnp.concatenate([hi, hi, lo], axis=1)


def right3(v):
    hi, lo = split3(v)
    return jnp.concatenate([hi, lo, hi], axis=0)


def mix(m, v):
    return jnp.dot(left3(m), right3(v), preferred_element_type=F32)


def fold(m):
    half = m.shape[0] // 2
    return jnp.concatenate([m[:half], m[half:]], axis=1)


def unfold(m):
    half = m.shape[1] // 2
    return jnp.concatenate([m[:, :half], m[:, half:]], axis=0)


def eye(n):
    return (
        lax.broadcasted_iota(jnp.int32, (n, n), 0) == lax.broadcasted_iota(jnp.int32, (n, n), 1)
    ).astype(F32)


def edge_kernel(g_ref, p_ref, k_ref, up_ref, down_ref, kv_ref, p_first, p_last, sems):
    end = g_ref.shape[3] - 128
    first, last = pl.ds(0, 128), pl.ds(end, 128)
    copies = [
        pltpu.make_async_copy(p_ref.at[:, 0, :, first], p_first, sems.at[0]),
        pltpu.make_async_copy(p_ref.at[:, 0, :, last], p_last, sems.at[1]),
        pltpu.make_async_copy(g_ref.at[0, 0, :, first], up_ref.at[pl.ds(0, 64)], sems.at[2]),
        pltpu.make_async_copy(g_ref.at[0, 0, :, last], down_ref.at[pl.ds(0, 64)], sems.at[3]),
        pltpu.make_async_copy(k_ref, kv_ref, sems.at[4]),
    ]
    for copy in copies:
        copy.start()
    for copy in copies:
        copy.wait()
    up_ref[64:] = jnp.concatenate([p_first[n].astype(F32)[:, :WIDTH] for n in range(2)], axis=1)
    down_ref[64:] = jnp.concatenate([p_last[n].astype(F32)[:, WIDTH:] for n in range(2)], axis=1)


def edges(guess, probes, kernels):
    held = [pltpu.with_memory_space_constraint(v, pltpu.HBM) for v in (guess, probes, kernels)]
    return pl.pallas_call(
        edge_kernel,
        in_specs=[pl.BlockSpec(memory_space=pltpu.HBM)] * 3,
        out_specs=[whole()] * 3,
        out_shape=[jax.ShapeDtypeStruct((128, 128), F32)] * 2
        + [jax.ShapeDtypeStruct(kernels.shape, BF16)],
        scratch_shapes=[pltpu.VMEM((2, 64, 128), BF16)] * 2 + [pltpu.SemaphoreType.DMA((5,))],
        compiler_params=pltpu.CompilerParams(vmem_limit_bytes=2 << 20),
        name="edges",
    )(*held)


def taps(v):
    n = v.shape[1]
    column = lax.broadcasted_iota(jnp.int32, (16, n), 1) & (WIDTH - 1)
    keep = [jnp.where(column == edge, 0.0, 1.0).astype(BF16) for edge in (WIDTH - 1, 0)]
    keep = [jnp.concatenate([k] * (v.shape[0] // 16), axis=0) for k in keep]
    left = pltpu.roll(v * keep[0], 1, 1)
    right = pltpu.roll(v * keep[1], n - 1, 1)
    rows = []
    for part in (left, v, right):
        above = pltpu.roll(part, WIDTH, 1)
        below = jnp.concatenate([above[:, 128:], above[:, :128]], axis=1)
        rows.append((above, part, below))
    return jnp.concatenate([rows[dx][dy] for dy in range(3) for dx in range(3)], axis=0)


def rounded(v):
    return v.astype(BF16).astype(F32)


def convolve(kernel, v, at=None):
    stack = taps(v.astype(BF16))
    return jnp.dot(kernel, stack if at is None else stack[:, at], preferred_element_type=F32)


def bias_of(b_ref, layer):
    return jnp.sum(
        jnp.where(eye(64) == 1.0, b_ref[layer : layer + 1, :], 0.0), axis=1, keepdims=True
    )


def side(ref, n):
    return ref[64:, n * WIDTH : (n + 1) * WIDTH]


def inner_kernel(place_ref, g_ref, p_ref, k_ref, b_ref, state_ref, offset_ref, change_ref, t_ref):
    leading = place_ref[0] == 0
    g = g_ref[0, 0]
    cells = g.shape[1]
    kernel = k_ref[0]
    activation = jnp.tanh(g)
    slopes = 1.0 - activation * activation
    forcing = STEP * (convolve(kernel, activation) + bias_of(b_ref, 0))
    total = jnp.zeros((64, cells), F32)
    for n in range(2):
        probe = p_ref[n, 0].astype(F32)
        total = total + probe * convolve(kernel, slopes * probe)
    lane = lax.broadcasted_iota(jnp.int32, (64, cells), 1)
    total = jnp.where((lane >= WIDTH) & (lane < cells - WIDTH), total, 0.0)
    t_ref[...] = jnp.full((8, 128), 0.5 * jnp.sum(total))
    both = k_ref[0].astype(F32) + k_ref[1].astype(F32)
    pair = both[:, :128] + both[:, 128:256] + both[:, 256:384] + both[:, 384:512]
    coarse = STEP * (pair[:, :64] + pair[:, 64:] + both[:, 512:])
    state_ref[...] = g + forcing
    offset_ref[...] = forcing + jnp.where(leading, g, -mix(coarse, g))
    change_ref[...] = fold(jnp.where(leading, -eye(64), coarse))


def outer_kernel(
    strips,
    strip_ref,
    g_ref,
    low_ref,
    high_ref,
    p_ref,
    k_ref,
    b_ref,
    state_ref,
    offset_ref,
    change_ref,
    inner_ref,
    send_ref,
    t_ref,
):
    cells = state_ref.shape[1]
    last = cells - 128
    zero = jnp.zeros((64, WIDTH), F32)
    ends = jnp.concatenate(
        [low_ref[:64], g_ref[0, 0, :, :128], g_ref[0, 0, :, last:], high_ref[:64]], axis=1
    )
    probe_mid = [p_ref[n, 0].astype(F32) for n in range(2)]
    activation = jnp.tanh(ends)
    slopes = 1.0 - activation * activation
    kernel = k_ref[0]
    forcing = STEP * (convolve(kernel, activation) + bias_of(b_ref, 0))
    total = jnp.zeros((64, 128), F32)
    for n in range(2):
        probe = jnp.concatenate(
            [
                zero,
                side(low_ref, n),
                probe_mid[n][:, :128],
                probe_mid[n][:, last:],
                side(high_ref, n),
                zero,
            ],
            axis=1,
        )
        found = convolve(kernel, slopes * probe, slice(128, 384))
        total = total + jnp.concatenate(
            [
                probe_mid[n][:, :WIDTH] * found[:, :WIDTH],
                probe_mid[n][:, last + WIDTH :] * found[:, 256 - WIDTH :],
            ],
            axis=1,
        )
    rows = lax.broadcasted_iota(jnp.int32, (8, 128), 0)
    trace = inner_ref[...] + 0.5 * jnp.sum(total)

    lane = lax.broadcasted_iota(jnp.int32, (64, 128), 1)
    fresh = ends + forcing
    first, final = state_ref[:, :128], state_ref[:, last:]
    new_first = jnp.where(lane < WIDTH, fresh[:, 128:256], first)
    new_final = jnp.where(lane < WIDTH, final, fresh[:, 256:384])
    current = jnp.concatenate(
        [fresh[:, :128], new_first, state_ref[:, 128:last], new_final, fresh[:, 384:]], axis=1
    )
    wide = cells + 256
    far_lane = lax.broadcasted_iota(jnp.int32, (64, wide), 1)
    outside = ((strip_ref[0] == 0) & (far_lane < 128)) | (
        (strip_ref[0] == strips - 1) & (far_lane >= wide - 128)
    )
    middle = slice(128, 128 + cells)
    activation = jnp.where(outside, 0.0, jnp.tanh(current))
    slopes = 1.0 - activation * activation
    kernel = k_ref[1]
    forcing = STEP * (convolve(kernel, activation, middle) + bias_of(b_ref, 1))
    total = jnp.zeros((64, cells), F32)
    for n in range(2):
        probe = jnp.concatenate(
            [zero, side(low_ref, n), probe_mid[n], side(high_ref, n), zero], axis=1
        )
        total = total + probe_mid[n] * convolve(kernel, slopes * probe, middle)
    trace = jnp.where(rows == 1, 0.5 * jnp.sum(total), jnp.where(rows == 0, trace, 0.0))
    t_ref[...] = trace
    for j in range(cells // 128):
        at = slice(j * 128, (j + 1) * 128)
        part = offset_ref[:, at] + forcing[:, at]
        if j == 0:
            part = part + (new_first - first)
        if j == cells // 128 - 1:
            part = part + (new_final - final)
        send_ref[j, :64] = VALUE_SCALE * part
        send_ref[j, 64:] = CHANGE_SCALE * change_ref[...]


def whole(*shape):
    return pl.BlockSpec(memory_space=pltpu.VMEM)


def scalars():
    return pl.BlockSpec(memory_space=pltpu.SMEM)


def call(kernel, shapes, places, args, name, room, cost=None):
    return pl.pallas_call(
        kernel,
        in_specs=[scalars()] * places + [whole()] * (len(args) - places),
        out_specs=[whole() if len(s) > 1 else scalars() for s in shapes],
        out_shape=[jax.ShapeDtypeStruct(s, F32) for s in shapes],
        compiler_params=pltpu.CompilerParams(vmem_limit_bytes=room << 20),
        cost_estimate=cost,
        name=name,
    )(*args)


def exponent(v):
    return jnp.ceil(jnp.log2(jnp.maximum(v, 1e-30)))


def block_exponent(v):
    return exponent(jnp.max(jnp.abs(v), axis=(0, 1), keepdims=True))


def scaled(v, power):
    return v * jnp.exp2(15.0 - power)


def restored(v, power):
    return v * jnp.exp2(power - 15.0)


def tags(t, value_power, change_power):
    lane = lax.broadcasted_iota(jnp.int32, (8, 128), 1)
    power = exponent(jnp.abs(t))
    unit = t * jnp.exp2(-power)
    coarse = rounded(unit)
    fine = 256.0 * (unit - coarse)
    scales = jnp.where(lane < 112, value_power, change_power)
    return jnp.where(
        lane < 32, coarse, jnp.where(lane < 64, fine, jnp.where(lane < 96, power, scales))
    )


def read_tags(r):
    t = (r[:, :1] + r[:, 32:33] / 256.0) * jnp.exp2(r[:, 64:65])
    return t, r[:1, 96:97], r[:1, 112:113]


def put(ref, change, value, t):
    value_power, change_power = block_exponent(value), block_exponent(change)
    value = scaled(value, value_power)
    change = scaled(fold(change), change_power)
    extra = tags(t, value_power, change_power)
    for i in range(ref.shape[0]):
        ref[i, :64] = value
        ref[i, 64:96] = change
        ref[i, 96:] = extra


def take(r):
    t, value_power, change_power = read_tags(r[96:])
    return unfold(restored(r[64:96], change_power)), restored(r[:64], value_power), t


def join(earlier, later):
    change, offset = later
    wide = jnp.concatenate([earlier[1], earlier[0]], axis=1)
    moved = wide + mix(change, wide)
    return moved[:, 128:] + change, moved[:, :128] + offset


def near_kernel(r_ref, t_ref, other_ref, send_ref, value_ref, matrix_ref):
    count = r_ref.shape[0]
    spans = [
        (unfold(r_ref[j, 64:] / CHANGE_SCALE), r_ref[j, :64] / VALUE_SCALE) for j in range(count)
    ]
    before = [None] + spans[:1]
    pairs = [join(spans[j], spans[j + 1]) for j in range(0, count, 2)]
    upto = pairs[:1]
    if count == 8:
        quads = [join(pairs[0], pairs[1]), join(pairs[2], pairs[3])]
        total = join(quads[0], quads[1])
        upto = [pairs[0], quads[0], join(quads[0], pairs[2])]
    else:
        total = join(pairs[0], pairs[1])
    for i, span in enumerate(upto):
        before += [span, join(span, spans[2 * i + 2])]
    for j in range(count):
        matrix, value = before[j] if j else (jnp.zeros((64, 64), F32), jnp.zeros((64, 128), F32))
        value_ref[j] = value
        matrix_ref[j] = matrix
    put(send_ref, *total, t_ref[...] + other_ref[...])


def far_kernel(place_ref, r_ref, send_ref, value_ref, matrix_ref):
    count = r_ref.shape[0]
    me = place_ref[0]
    span = own = (jnp.zeros((64, 64), F32), jnp.zeros((64, 128), F32))
    before = total = mine = jnp.zeros((8, 1), F32)
    for i in range(count):
        own = tuple(jnp.where(me == i, new, old) for new, old in zip(span, own))
        change, value, t = take(r_ref[i])
        before = jnp.where(me == i, total, before)
        mine = jnp.where(me == i, t, mine)
        total = total + t
        span = join(span, (change, value)) if i else (change, value)
    matrix_ref[...], value_ref[...] = own
    spread = jnp.sum(before, axis=0, keepdims=True)
    t = jnp.concatenate([total[:2], mine[:2], spread, jnp.zeros((3, 1), F32)], axis=0)
    put(send_ref, *span, jnp.broadcast_to(t, (8, 128)))


def back_kernel(
    place_ref, strip_ref, r_ref, far_value, far_matrix, near_value, near_matrix, send_ref
):
    me, strip = place_ref[0], strip_ref[0]
    state = own = jnp.zeros((64, 128), F32)
    before = total = mine = jnp.zeros((8, 1), F32)
    copies = 2
    count = r_ref.shape[0] // copies
    for i in range(count):
        own = jnp.where(me == i, state, own)
        before = jnp.where(me == i, total, before)
        t = sum(read_tags(r_ref[copies * i + n, 96:])[0] for n in range(copies))
        mine = jnp.where(me == i, t, mine)
        total = total + t
        if i < count - 1:
            change, value, _ = take(r_ref[copies * i + strip])
            state = state + mix(change, state) + value
    entry = own + mix(far_matrix[...], own) + far_value[...]
    near = near_matrix.shape[0]
    states = mix(near_matrix[...].reshape(near * 64, 64), entry)
    spread = jnp.sum(before[:2], axis=0, keepdims=True)
    t = jnp.concatenate([mine[2:5], spread, jnp.zeros((4, 1), F32)], axis=0)
    t = jnp.broadcast_to(t, (8, 128))
    states = [entry + states[j * 64 : (j + 1) * 64] + near_value[j] for j in range(near)]
    power = block_exponent(functools.reduce(jnp.maximum, [jnp.abs(state) for state in states]))
    extra = tags(t, power, power)
    for j in range(near):
        send_ref[j, :64] = scaled(states[j], power)
        send_ref[j, 64:] = extra


def final_kernel(place_ref, me_ref, r_ref, g_ref, state_ref, log_ref):
    leading, me = place_ref[0] == 0, me_ref[0]
    count = r_ref.shape[0]
    earlier = jnp.zeros((1, 1), F32)
    own = jnp.zeros((8, 1), F32)
    for j in range(count):
        at = slice(j * 128, (j + 1) * 128)
        t, power, _ = read_tags(r_ref[j, 64:])
        state = restored(r_ref[j, :64], power)
        state_ref[0, 0, :, at] = jnp.where(leading, g_ref[0, 0, :, at], state)
        earlier = earlier + t[2:3] + t[3:4] + jnp.where(j < me, t[0:1] + t[1:2], 0.0)
        own = jnp.where(me == j, t, own)
    first = earlier + own[0:1]
    second = first + own[1:2]
    log_ref[0] = -(STEP / WIDTH) * first[0, 0]
    log_ref[1] = -(STEP / WIDTH) * second[0, 0]


def exchange(v, axes):
    return lax.all_to_all(v.astype(F16), axes, 0, 0, tiled=True).astype(F32)


def body(guess, kernels, biases, probes):
    strips = lax.axis_size(SPACE)
    strip = lax.axis_index(SPACE)
    near = lax.axis_size(NEAR)
    far, last = lax.axis_size("zh"), lax.axis_size("x")
    cells = guess.shape[3]
    place = lax.axis_index(TM).reshape(1)

    up, down, kernels = edges(guess, probes, kernels)
    forward = [(i, i + 1) for i in range(strips - 1)]
    backward = [(i + 1, i) for i in range(strips - 1)]
    low = lax.ppermute(down, SPACE, forward)
    high = lax.ppermute(up, SPACE, backward)
    state, offset, change, inner = call(
        inner_kernel,
        [(64, cells), (64, cells), (32, 128), (8, 128)],
        1,
        (place, guess, probes, kernels, biases),
        "inner",
        20,
        pl.CostEstimate(flops=450_000_000, bytes_accessed=2_000_000, transcendentals=65536),
    )
    send, trace = call(
        functools.partial(outer_kernel, strips),
        [(near, 96, 128), (8, 128)],
        1,
        (
            strip.reshape(1), guess, low, high, probes, kernels, biases,
            state, offset, change, inner,
        ),
        "outer",
        20,
    )
    got = exchange(send, NEAR)
    other = lax.ppermute(trace, "sl", [(0, 1), (1, 0)])
    send, near_value, near_matrix = call(
        near_kernel,
        [(far, 104, 128), (near, 64, 128), (near, 64, 64)],
        0,
        (got, trace, other),
        "near",
        8,
    )
    got = exchange(send, "zh")
    send, far_value, far_matrix = call(
        far_kernel,
        [(2 * last, 104, 128), (64, 128), (64, 64)],
        1,
        (lax.axis_index("zh").reshape(1), got),
        "far",
        8,
    )
    got = exchange(send, ("x", "sh"))
    (send,) = call(
        back_kernel,
        [(near, 72, 128)],
        2,
        (
            lax.axis_index("x").reshape(1),
            lax.axis_index("sh").reshape(1),
            got,
            far_value,
            far_matrix,
            near_value,
            near_matrix,
        ),
        "back",
        8,
    )
    got = exchange(send, NEAR)
    return call(
        final_kernel,
        [(1, 1, 64, cells), (2,)],
        2,
        (place, lax.axis_index(NEAR).reshape(1), got, guess),
        "final",
        8,
    )


def solution(mesh):
    finer = Mesh(
        mesh.devices.reshape(4, 4, 4, 2, 2, 2), ("x", "zh", "zl", "c", "sh", "sl")
    )
    placed = (
        P(TM, None, None, SPACE),
        P(TM, None, None),
        P(TM, None),
        P(None, None, None, SPACE),
    )
    return jax.shard_map(
        body,
        mesh=finer,
        in_specs=placed,
        out_specs=(P(TM, None, None, SPACE), P(TM)),
        check_vma=False,
    )
```

```python
import functools

import jax
import jax.numpy as jnp
from jax import lax
from jax.experimental import pallas as pl
from jax.experimental.pallas import tpu as pltpu
from jax.sharding import Mesh
from jax.sharding import PartitionSpec as P

WIDTH = 64
STEP = 0.0078125
TM = ("x", "zh", "zl", "c")
NEAR = ("zl", "c")
SPACE = ("sh", "sl")
VALUE_SCALE = 2048.0
CHANGE_SCALE = 32768.0
F16 = jnp.float16
F32 = jnp.float32
BF16 = jnp.bfloat16


def split3(m):
    hi = m.astype(BF16)
    return hi, (m - hi.astype(F32)).astype(BF16)


def left3(m):
    hi, lo = split3(m)
    return jnp.concatenate([hi, hi, lo], axis=1)


def right3(v):
    hi, lo = split3(v)
    return jnp.concatenate([hi, lo, hi], axis=0)


def mix(m, v):
    return jnp.dot(left3(m), right3(v), preferred_element_type=F32)


def fold(m):
    half = m.shape[0] // 2
    return jnp.concatenate([m[:half], m[half:]], axis=1)


def unfold(m):
    half = m.shape[1] // 2
    return jnp.concatenate([m[:, :half], m[:, half:]], axis=0)


def eye(n):
    return (
        lax.broadcasted_iota(jnp.int32, (n, n), 0) == lax.broadcasted_iota(jnp.int32, (n, n), 1)
    ).astype(F32)


def edge_kernel(g_ref, p_ref, k_ref, up_ref, down_ref, kv_ref, p_first, p_last, sems):
    end = g_ref.shape[3] - 128
    first, last = pl.ds(0, 128), pl.ds(end, 128)
    copies = [
        pltpu.make_async_copy(p_ref.at[:, 0, :, first], p_first, sems.at[0]),
        pltpu.make_async_copy(p_ref.at[:, 0, :, last], p_last, sems.at[1]),
        pltpu.make_async_copy(g_ref.at[0, 0, :, first], up_ref.at[pl.ds(0, 64)], sems.at[2]),
        pltpu.make_async_copy(g_ref.at[0, 0, :, last], down_ref.at[pl.ds(0, 64)], sems.at[3]),
        pltpu.make_async_copy(k_ref, kv_ref, sems.at[4]),
    ]
    for copy in copies:
        copy.start()
    for copy in copies:
        copy.wait()
    up_ref[64:] = jnp.concatenate([p_first[n].astype(F32)[:, :WIDTH] for n in range(2)], axis=1)
    down_ref[64:] = jnp.concatenate([p_last[n].astype(F32)[:, WIDTH:] for n in range(2)], axis=1)


def edges(guess, probes, kernels):
    held = [pltpu.with_memory_space_constraint(v, pltpu.HBM) for v in (guess, probes, kernels)]
    return pl.pallas_call(
        edge_kernel,
        in_specs=[pl.BlockSpec(memory_space=pltpu.HBM)] * 3,
        out_specs=[whole()] * 3,
        out_shape=[jax.ShapeDtypeStruct((128, 128), F32)] * 2
        + [jax.ShapeDtypeStruct(kernels.shape, BF16)],
        scratch_shapes=[pltpu.VMEM((2, 64, 128), BF16)] * 2 + [pltpu.SemaphoreType.DMA((5,))],
        compiler_params=pltpu.CompilerParams(vmem_limit_bytes=2 << 20),
        name="edges",
    )(*held)


def taps(v):
    n = v.shape[1]
    column = lax.broadcasted_iota(jnp.int32, (16, n), 1) & (WIDTH - 1)
    keep = [jnp.where(column == edge, 0.0, 1.0).astype(BF16) for edge in (WIDTH - 1, 0)]
    keep = [jnp.concatenate([k] * (v.shape[0] // 16), axis=0) for k in keep]
    left = pltpu.roll(v * keep[0], 1, 1)
    right = pltpu.roll(v * keep[1], n - 1, 1)
    rows = []
    for part in (left, v, right):
        above = pltpu.roll(part, WIDTH, 1)
        below = jnp.concatenate([above[:, 128:], above[:, :128]], axis=1)
        rows.append((above, part, below))
    return jnp.concatenate([rows[dx][dy] for dy in range(3) for dx in range(3)], axis=0)


def rounded(v):
    return v.astype(BF16).astype(F32)


def convolve(kernel, v, at=None):
    stack = taps(v.astype(BF16))
    return jnp.dot(kernel, stack if at is None else stack[:, at], preferred_element_type=F32)


def bias_of(b_ref, layer):
    return jnp.sum(
        jnp.where(eye(64) == 1.0, b_ref[layer : layer + 1, :], 0.0), axis=1, keepdims=True
    )


def side(ref, n):
    return ref[64:, n * WIDTH : (n + 1) * WIDTH]


def inner_kernel(place_ref, g_ref, p_ref, k_ref, b_ref, state_ref, offset_ref, change_ref, t_ref):
    leading = place_ref[0] == 0
    g = g_ref[0, 0]
    cells = g.shape[1]
    kernel = k_ref[0]
    activation = jnp.tanh(g)
    slopes = 1.0 - activation * activation
    forcing = STEP * (convolve(kernel, activation) + bias_of(b_ref, 0))
    total = jnp.zeros((64, cells), F32)
    for n in range(2):
        probe = p_ref[n, 0].astype(F32)
        total = total + probe * convolve(kernel, slopes * probe)
    lane = lax.broadcasted_iota(jnp.int32, (64, cells), 1)
    total = jnp.where((lane >= WIDTH) & (lane < cells - WIDTH), total, 0.0)
    t_ref[...] = jnp.full((8, 128), 0.5 * jnp.sum(total))
    both = k_ref[0].astype(F32) + k_ref[1].astype(F32)
    pair = both[:, :128] + both[:, 128:256] + both[:, 256:384] + both[:, 384:512]
    coarse = STEP * (pair[:, :64] + pair[:, 64:] + both[:, 512:])
    state_ref[...] = g + forcing
    offset_ref[...] = forcing + jnp.where(leading, g, -mix(coarse, g))
    change_ref[...] = fold(jnp.where(leading, -eye(64), coarse))


def outer_kernel(
    strips,
    strip_ref,
    g_ref,
    low_ref,
    high_ref,
    p_ref,
    k_ref,
    b_ref,
    state_ref,
    offset_ref,
    change_ref,
    inner_ref,
    send_ref,
    t_ref,
):
    cells = state_ref.shape[1]
    last = cells - 128
    zero = jnp.zeros((64, WIDTH), F32)
    ends = jnp.concatenate(
        [low_ref[:64], g_ref[0, 0, :, :128], g_ref[0, 0, :, last:], high_ref[:64]], axis=1
    )
    probe_mid = [p_ref[n, 0].astype(F32) for n in range(2)]
    activation = jnp.tanh(ends)
    slopes = 1.0 - activation * activation
    kernel = k_ref[0]
    forcing = STEP * (convolve(kernel, activation) + bias_of(b_ref, 0))
    total = jnp.zeros((64, 128), F32)
    for n in range(2):
        probe = jnp.concatenate(
            [
                zero,
                side(low_ref, n),
                probe_mid[n][:, :128],
                probe_mid[n][:, last:],
                side(high_ref, n),
                zero,
            ],
            axis=1,
        )
        found = convolve(kernel, slopes * probe, slice(128, 384))
        total = total + jnp.concatenate(
            [
                probe_mid[n][:, :WIDTH] * found[:, :WIDTH],
                probe_mid[n][:, last + WIDTH :] * found[:, 256 - WIDTH :],
            ],
            axis=1,
        )
    rows = lax.broadcasted_iota(jnp.int32, (8, 128), 0)
    trace = inner_ref[...] + 0.5 * jnp.sum(total)

    lane = lax.broadcasted_iota(jnp.int32, (64, 128), 1)
    fresh = ends + forcing
    first, final = state_ref[:, :128], state_ref[:, last:]
    new_first = jnp.where(lane < WIDTH, fresh[:, 128:256], first)
    new_final = jnp.where(lane < WIDTH, final, fresh[:, 256:384])
    current = jnp.concatenate(
        [fresh[:, :128], new_first, state_ref[:, 128:last], new_final, fresh[:, 384:]], axis=1
    )
    wide = cells + 256
    far_lane = lax.broadcasted_iota(jnp.int32, (64, wide), 1)
    outside = ((strip_ref[0] == 0) & (far_lane < 128)) | (
        (strip_ref[0] == strips - 1) & (far_lane >= wide - 128)
    )
    middle = slice(128, 128 + cells)
    activation = jnp.where(outside, 0.0, jnp.tanh(current))
    slopes = 1.0 - activation * activation
    kernel = k_ref[1]
    forcing = STEP * (convolve(kernel, activation, middle) + bias_of(b_ref, 1))
    total = jnp.zeros((64, cells), F32)
    for n in range(2):
        probe = jnp.concatenate(
            [zero, side(low_ref, n), probe_mid[n], side(high_ref, n), zero], axis=1
        )
        total = total + probe_mid[n] * convolve(kernel, slopes * probe, middle)
    trace = jnp.where(rows == 1, 0.5 * jnp.sum(total), jnp.where(rows == 0, trace, 0.0))
    t_ref[...] = trace
    for j in range(cells // 128):
        at = slice(j * 128, (j + 1) * 128)
        part = offset_ref[:, at] + forcing[:, at]
        if j == 0:
            part = part + (new_first - first)
        if j == cells // 128 - 1:
            part = part + (new_final - final)
        send_ref[j, :64] = VALUE_SCALE * part
        send_ref[j, 64:] = CHANGE_SCALE * change_ref[...]


def whole(*shape):
    return pl.BlockSpec(memory_space=pltpu.VMEM)


def scalars():
    return pl.BlockSpec(memory_space=pltpu.SMEM)


def call(kernel, shapes, places, args, name, room, cost=None):
    return pl.pallas_call(
        kernel,
        in_specs=[scalars()] * places + [whole()] * (len(args) - places),
        out_specs=[whole() if len(s) > 1 else scalars() for s in shapes],
        out_shape=[jax.ShapeDtypeStruct(s, F32) for s in shapes],
        compiler_params=pltpu.CompilerParams(vmem_limit_bytes=room << 20),
        cost_estimate=cost,
        name=name,
    )(*args)


def exponent(v):
    return jnp.ceil(jnp.log2(jnp.maximum(v, 1e-30)))


def block_exponent(v):
    return exponent(jnp.max(jnp.abs(v), axis=(0, 1), keepdims=True))


def scaled(v, power):
    return v * jnp.exp2(15.0 - power)


def restored(v, power):
    return v * jnp.exp2(power - 15.0)


def tags(t, value_power, change_power):
    lane = lax.broadcasted_iota(jnp.int32, (8, 128), 1)
    power = exponent(jnp.abs(t))
    unit = t * jnp.exp2(-power)
    coarse = rounded(unit)
    fine = 256.0 * (unit - coarse)
    scales = jnp.where(lane < 112, value_power, change_power)
    return jnp.where(
        lane < 32, coarse, jnp.where(lane < 64, fine, jnp.where(lane < 96, power, scales))
    )


def read_tags(r):
    t = (r[:, :1] + r[:, 32:33] / 256.0) * jnp.exp2(r[:, 64:65])
    return t, r[:1, 96:97], r[:1, 112:113]


def put(ref, change, value, t):
    value_power, change_power = block_exponent(value), block_exponent(change)
    value = scaled(value, value_power)
    change = scaled(fold(change), change_power)
    extra = tags(t, value_power, change_power)
    for i in range(ref.shape[0]):
        ref[i, :64] = value
        ref[i, 64:96] = change
        ref[i, 96:] = extra


def take(r):
    t, value_power, change_power = read_tags(r[96:])
    return unfold(restored(r[64:96], change_power)), restored(r[:64], value_power), t


def join(earlier, later):
    change, offset = later
    wide = jnp.concatenate([earlier[1], earlier[0]], axis=1)
    moved = wide + mix(change, wide)
    return moved[:, 128:] + change, moved[:, :128] + offset


def near_kernel(r_ref, t_ref, other_ref, send_ref, value_ref, matrix_ref):
    count = r_ref.shape[0]
    spans = [
        (unfold(r_ref[j, 64:] / CHANGE_SCALE), r_ref[j, :64] / VALUE_SCALE) for j in range(count)
    ]
    before = [None] + spans[:1]
    pairs = [join(spans[j], spans[j + 1]) for j in range(0, count, 2)]
    upto = pairs[:1]
    if count == 8:
        quads = [join(pairs[0], pairs[1]), join(pairs[2], pairs[3])]
        total = join(quads[0], quads[1])
        upto = [pairs[0], quads[0], join(quads[0], pairs[2])]
    else:
        total = join(pairs[0], pairs[1])
    for i, span in enumerate(upto):
        before += [span, join(span, spans[2 * i + 2])]
    for j in range(count):
        matrix, value = before[j] if j else (jnp.zeros((64, 64), F32), jnp.zeros((64, 128), F32))
        value_ref[j] = value
        matrix_ref[j] = matrix
    put(send_ref, *total, t_ref[...] + other_ref[...])


def far_kernel(place_ref, r_ref, send_ref, value_ref, matrix_ref):
    count = r_ref.shape[0]
    me = place_ref[0]
    spans, traces = [], []
    for i in range(count):
        change, value, t = take(r_ref[i])
        spans.append((change, value))
        traces.append(t)
    upto = [(jnp.zeros((64, 64), F32), jnp.zeros((64, 128), F32)), spans[0]]
    upto.append(join(spans[0], spans[1]))
    if count == 4:
        upto.append(join(upto[2], spans[2]))
        upto.append(join(upto[2], join(spans[2], spans[3])))
    own = upto[0]
    before = total = mine = jnp.zeros((8, 1), F32)
    for i in range(count):
        own = tuple(jnp.where(me == i, new, old) for new, old in zip(upto[i], own))
        before = jnp.where(me == i, total, before)
        mine = jnp.where(me == i, traces[i], mine)
        total = total + traces[i]
    matrix_ref[...], value_ref[...] = own
    spread = jnp.sum(before, axis=0, keepdims=True)
    t = jnp.concatenate([total[:2], mine[:2], spread, jnp.zeros((3, 1), F32)], axis=0)
    put(send_ref, *upto[count], jnp.broadcast_to(t, (8, 128)))


def back_kernel(
    place_ref, strip_ref, r_ref, far_value, far_matrix, near_value, near_matrix, send_ref
):
    me, strip = place_ref[0], strip_ref[0]
    state = own = jnp.zeros((64, 128), F32)
    before = total = mine = jnp.zeros((8, 1), F32)
    copies = 2
    count = r_ref.shape[0] // copies
    for i in range(count):
        own = jnp.where(me == i, state, own)
        before = jnp.where(me == i, total, before)
        t = sum(read_tags(r_ref[copies * i + n, 96:])[0] for n in range(copies))
        mine = jnp.where(me == i, t, mine)
        total = total + t
        if i < count - 1:
            change, value, _ = take(r_ref[copies * i + strip])
            state = state + mix(change, state) + value if i else value
    entry = own + mix(far_matrix[...], own) + far_value[...]
    near = near_matrix.shape[0]
    states = mix(near_matrix[...].reshape(near * 64, 64), entry)
    spread = jnp.sum(before[:2], axis=0, keepdims=True)
    t = jnp.concatenate([mine[2:5], spread, jnp.zeros((4, 1), F32)], axis=0)
    t = jnp.broadcast_to(t, (8, 128))
    states = [entry + states[j * 64 : (j + 1) * 64] + near_value[j] for j in range(near)]
    power = block_exponent(functools.reduce(jnp.maximum, [jnp.abs(state) for state in states]))
    extra = tags(t, power, power)
    for j in range(near):
        send_ref[j, :64] = scaled(states[j], power)
        send_ref[j, 64:] = extra


def final_kernel(place_ref, me_ref, r_ref, g_ref, state_ref, log_ref):
    leading, me = place_ref[0] == 0, me_ref[0]
    count = r_ref.shape[0]
    earlier = jnp.zeros((1, 1), F32)
    own = jnp.zeros((8, 1), F32)
    for j in range(count):
        at = slice(j * 128, (j + 1) * 128)
        t, power, _ = read_tags(r_ref[j, 64:])
        state = restored(r_ref[j, :64], power)
        state_ref[0, 0, :, at] = jnp.where(leading, g_ref[0, 0, :, at], state)
        earlier = earlier + t[2:3] + t[3:4] + jnp.where(j < me, t[0:1] + t[1:2], 0.0)
        own = jnp.where(me == j, t, own)
    first = earlier + own[0:1]
    second = first + own[1:2]
    log_ref[0] = -(STEP / WIDTH) * first[0, 0]
    log_ref[1] = -(STEP / WIDTH) * second[0, 0]


def exchange(v, axes):
    return lax.all_to_all(v.astype(F16), axes, 0, 0, tiled=True).astype(F32)


def body(guess, kernels, biases, probes):
    strips = lax.axis_size(SPACE)
    strip = lax.axis_index(SPACE)
    near = lax.axis_size(NEAR)
    far, last = lax.axis_size("zh"), lax.axis_size("x")
    cells = guess.shape[3]
    place = lax.axis_index(TM).reshape(1)

    up, down, kernels = edges(guess, probes, kernels)
    forward = [(i, i + 1) for i in range(strips - 1)]
    backward = [(i + 1, i) for i in range(strips - 1)]
    low = lax.ppermute(down, SPACE, forward)
    high = lax.ppermute(up, SPACE, backward)
    state, offset, change, inner = call(
        inner_kernel,
        [(64, cells), (64, cells), (32, 128), (8, 128)],
        1,
        (place, guess, probes, kernels, biases),
        "inner",
        20,
        pl.CostEstimate(flops=450_000_000, bytes_accessed=2_000_000, transcendentals=65536),
    )
    send, trace = call(
        functools.partial(outer_kernel, strips),
        [(near, 96, 128), (8, 128)],
        1,
        (
            strip.reshape(1), guess, low, high, probes, kernels, biases,
            state, offset, change, inner,
        ),
        "outer",
        20,
    )
    got = exchange(send, NEAR)
    across = [(i, i ^ 1) for i in range(strips)]
    other = lax.ppermute(
        trace, SPACE, [((i + 1) % strips, (j + 1) % strips) for i, j in across]
    )
    send, near_value, near_matrix = call(
        near_kernel,
        [(far, 104, 128), (near, 64, 128), (near, 64, 64)],
        0,
        (got, trace, other),
        "near",
        8,
    )
    got = exchange(send, "zh")
    send, far_value, far_matrix = call(
        far_kernel,
        [(2 * last, 104, 128), (64, 128), (64, 64)],
        1,
        (lax.axis_index("zh").reshape(1), got),
        "far",
        8,
    )
    got = exchange(send, ("x", "sl"))
    (send,) = call(
        back_kernel,
        [(near, 72, 128)],
        2,
        (
            lax.axis_index("x").reshape(1),
            lax.axis_index("sl").reshape(1),
            got,
            far_value,
            far_matrix,
            near_value,
            near_matrix,
        ),
        "back",
        8,
    )
    got = exchange(send, NEAR)
    return call(
        final_kernel,
        [(1, 1, 64, cells), (2,)],
        2,
        (place, lax.axis_index(NEAR).reshape(1), got, guess),
        "final",
        8,
    )


def solution(mesh):
    finer = Mesh(
        mesh.devices.reshape(4, 4, 4, 2, 2, 2), ("x", "zh", "zl", "c", "sh", "sl")
    )
    placed = (
        P(TM, None, None, SPACE),
        P(TM, None, None),
        P(TM, None),
        P(None, None, None, SPACE),
    )
    return jax.shard_map(
        body,
        mesh=finer,
        in_specs=placed,
        out_specs=(P(TM, None, None, SPACE), P(TM)),
        check_vma=False,
    )
```

```python
import functools

import jax
import jax.numpy as jnp
from jax import lax
from jax.experimental import pallas as pl
from jax.experimental.pallas import tpu as pltpu
from jax.sharding import Mesh
from jax.sharding import PartitionSpec as P

WIDTH = 64
STEP = 0.0078125
TM = ("x", "zh", "zl", "c")
NEAR = ("zl", "c")
SPACE = ("sh", "sl")
VALUE_SCALE = 2048.0
CHANGE_SCALE = 32768.0
F16 = jnp.float16
F32 = jnp.float32
BF16 = jnp.bfloat16


def split3(m):
    hi = m.astype(BF16)
    return hi, (m - hi.astype(F32)).astype(BF16)


def left3(m):
    hi, lo = split3(m)
    return jnp.concatenate([hi, hi, lo], axis=1)


def right3(v):
    hi, lo = split3(v)
    return jnp.concatenate([hi, lo, hi], axis=0)


def mix(m, v):
    return jnp.dot(left3(m), right3(v), preferred_element_type=F32)


def fold(m):
    half = m.shape[0] // 2
    return jnp.concatenate([m[:half], m[half:]], axis=1)


def unfold(m):
    half = m.shape[1] // 2
    return jnp.concatenate([m[:, :half], m[:, half:]], axis=0)


def eye(n):
    return (
        lax.broadcasted_iota(jnp.int32, (n, n), 0) == lax.broadcasted_iota(jnp.int32, (n, n), 1)
    ).astype(F32)


def edge_kernel(g_ref, p_ref, k_ref, up_ref, down_ref, kv_ref, p_first, p_last, sems):
    end = g_ref.shape[3] - 128
    first, last = pl.ds(0, 128), pl.ds(end, 128)
    copies = [
        pltpu.make_async_copy(p_ref.at[:, 0, :, first], p_first, sems.at[0]),
        pltpu.make_async_copy(p_ref.at[:, 0, :, last], p_last, sems.at[1]),
        pltpu.make_async_copy(g_ref.at[0, 0, :, first], up_ref.at[pl.ds(0, 64)], sems.at[2]),
        pltpu.make_async_copy(g_ref.at[0, 0, :, last], down_ref.at[pl.ds(0, 64)], sems.at[3]),
        pltpu.make_async_copy(k_ref, kv_ref, sems.at[4]),
    ]
    for copy in copies:
        copy.start()
    for copy in copies:
        copy.wait()
    up_ref[64:] = jnp.concatenate([p_first[n].astype(F32)[:, :WIDTH] for n in range(2)], axis=1)
    down_ref[64:] = jnp.concatenate([p_last[n].astype(F32)[:, WIDTH:] for n in range(2)], axis=1)


def edges(guess, probes, kernels):
    held = [pltpu.with_memory_space_constraint(v, pltpu.HBM) for v in (guess, probes, kernels)]
    return pl.pallas_call(
        edge_kernel,
        in_specs=[pl.BlockSpec(memory_space=pltpu.HBM)] * 3,
        out_specs=[whole()] * 3,
        out_shape=[jax.ShapeDtypeStruct((128, 128), F32)] * 2
        + [jax.ShapeDtypeStruct(kernels.shape, BF16)],
        scratch_shapes=[pltpu.VMEM((2, 64, 128), BF16)] * 2 + [pltpu.SemaphoreType.DMA((5,))],
        compiler_params=pltpu.CompilerParams(vmem_limit_bytes=2 << 20),
        name="edges",
    )(*held)


def taps(v, closed=False):
    n = v.shape[1]
    column = lax.broadcasted_iota(jnp.int32, (16, n), 1) & (WIDTH - 1)
    keep = [jnp.where(column == edge, 0.0, 1.0).astype(BF16) for edge in (WIDTH - 1, 0)]
    keep = [jnp.concatenate([k] * (v.shape[0] // 16), axis=0) for k in keep]
    left = pltpu.roll(v * keep[0], 1, 1)
    right = pltpu.roll(v * keep[1], n - 1, 1)
    lane = lax.broadcasted_iota(jnp.int32, (v.shape[0], 128), 1)
    low = jnp.where(lane < WIDTH, 1.0, 0.0).astype(BF16)
    high = jnp.where(lane < WIDTH, 0.0, 1.0).astype(BF16)
    rows = []
    for part in (left, v, right):
        above = pltpu.roll(part, WIDTH, 1)
        below = jnp.concatenate([above[:, 128:], above[:, :128]], axis=1)
        if closed:
            above = jnp.concatenate([above[:, :128] * high, above[:, 128:]], axis=1)
            below = jnp.concatenate([below[:, : n - 128], below[:, n - 128 :] * low], axis=1)
        rows.append((above, part, below))
    return jnp.concatenate([rows[dx][dy] for dy in range(3) for dx in range(3)], axis=0)


def rounded(v):
    return v.astype(BF16).astype(F32)


def convolve(kernel, v, at=None):
    stack = taps(v.astype(BF16))
    return jnp.dot(kernel, stack if at is None else stack[:, at], preferred_element_type=F32)


def bias_of(b_ref, layer):
    return jnp.sum(
        jnp.where(eye(64) == 1.0, b_ref[layer : layer + 1, :], 0.0), axis=1, keepdims=True
    )


def adjoint(k_ref):
    blocks = []
    for at in range(0, 9 * 64, 128):
        both = jnp.concatenate([k_ref[n, :, at : at + 128].astype(F32) for n in range(2)], axis=0)
        turned = both.T
        blocks += [turned[i : i + 64] for i in range(0, turned.shape[0], 64)]
    blocks = blocks[::-1]
    return jnp.concatenate(
        [
            jnp.concatenate([block[:, n * 64 : (n + 1) * 64] for block in blocks], axis=1)
            for n in range(2)
        ],
        axis=0,
    ).astype(BF16)


def inner_kernel(
    place_ref, g_ref, p_ref, k_ref, b_ref, state_ref, offset_ref, change_ref, t_ref, pull_ref, a_ref
):
    leading = place_ref[0] == 0
    g = g_ref[0, 0]
    activation = jnp.tanh(g)
    slopes = 1.0 - activation * activation
    forcing = STEP * (convolve(k_ref[0], activation) + bias_of(b_ref, 0))
    turned = adjoint(k_ref)
    a_ref[...] = turned
    total = jnp.zeros(g.shape, F32)
    for n in range(2):
        probe = p_ref[n, 0]
        pulled = jnp.dot(turned, taps(probe, True), preferred_element_type=F32)
        total = total + pulled[:64] * rounded(slopes * probe.astype(F32))
        pull_ref[n] = pulled[64:]
    t_ref[...] = jnp.full((8, 128), 0.5 * jnp.sum(total))
    both = k_ref[0].astype(F32) + k_ref[1].astype(F32)
    pair = both[:, :128] + both[:, 128:256] + both[:, 256:384] + both[:, 384:512]
    coarse = STEP * (pair[:, :64] + pair[:, 64:] + both[:, 512:])
    state_ref[...] = g + forcing
    offset_ref[...] = forcing + jnp.where(leading, g, -mix(coarse, g))
    change_ref[...] = fold(jnp.where(leading, -eye(64), coarse))


def sides(v):
    column = lax.broadcasted_iota(jnp.int32, v.shape, 1) & (WIDTH - 1)
    left = pltpu.roll(jnp.where(column == WIDTH - 1, 0.0, v), 1, 1)
    right = pltpu.roll(jnp.where(column == 0, 0.0, v), v.shape[1] - 1, 1)
    return jnp.concatenate([left, v, right], axis=0).astype(BF16)


def twice(v, at):
    return jnp.concatenate([v[:, at : at + WIDTH]] * 2, axis=1)


def outer_kernel(
    strips,
    strip_ref,
    g_ref,
    low_ref,
    high_ref,
    p_ref,
    k_ref,
    b_ref,
    state_ref,
    offset_ref,
    change_ref,
    inner_ref,
    pull_ref,
    a_ref,
    send_ref,
    t_ref,
):
    cells = state_ref.shape[1]
    last = cells - 128
    ends = jnp.concatenate(
        [low_ref[:64], g_ref[0, 0, :, :128], g_ref[0, 0, :, last:], high_ref[:64]], axis=1
    )
    probe_mid = [p_ref[n, 0].astype(F32) for n in range(2)]
    activation = jnp.tanh(ends)
    end_slopes = 1.0 - activation * activation
    forcing = STEP * (convolve(k_ref[0], activation) + bias_of(b_ref, 0))

    turned = a_ref[...]
    pulls = [
        jnp.dot(turned[:, :192], sides(low_ref[64:]), preferred_element_type=F32),
        jnp.dot(turned[:, 384:], sides(high_ref[64:]), preferred_element_type=F32),
    ]
    edge_probe = [
        jnp.concatenate([v[:, :WIDTH] for v in probe_mid], axis=1),
        jnp.concatenate([v[:, cells - WIDTH :] for v in probe_mid], axis=1),
    ]
    total = sum(
        pulls[i][:64] * rounded(twice(end_slopes, (128, 320)[i]) * edge_probe[i]) for i in range(2)
    )
    trace = inner_ref[...] + 0.5 * jnp.sum(total)

    lane = lax.broadcasted_iota(jnp.int32, (64, 128), 1)
    fresh = ends + forcing
    first, final = state_ref[:, :128], state_ref[:, last:]
    new_first = jnp.where(lane < WIDTH, fresh[:, 128:256], first)
    new_final = jnp.where(lane < WIDTH, final, fresh[:, 256:384])
    current = jnp.concatenate(
        [fresh[:, :128], new_first, state_ref[:, 128:last], new_final, fresh[:, 384:]], axis=1
    )
    wide = cells + 256
    far_lane = lax.broadcasted_iota(jnp.int32, (64, wide), 1)
    outside = ((strip_ref[0] == 0) & (far_lane < 128)) | (
        (strip_ref[0] == strips - 1) & (far_lane >= wide - 128)
    )
    activation = jnp.where(outside, 0.0, jnp.tanh(current))
    forcing = convolve(k_ref[1], activation, slice(128, 128 + cells))
    forcing = STEP * (forcing + bias_of(b_ref, 1))
    middle = activation[:, 128 : 128 + cells]
    slopes = 1.0 - middle * middle
    total = sum(pull_ref[n] * rounded(slopes * probe_mid[n]) for n in range(2))
    edge = sum(
        pulls[i][64:] * rounded(twice(slopes, (0, cells - WIDTH)[i]) * edge_probe[i])
        for i in range(2)
    )
    rows = lax.broadcasted_iota(jnp.int32, (8, 128), 0)
    second = 0.5 * (jnp.sum(total) + jnp.sum(edge))
    t_ref[...] = jnp.where(rows == 1, second, jnp.where(rows == 0, trace, 0.0))
    for j in range(cells // 128):
        at = slice(j * 128, (j + 1) * 128)
        part = offset_ref[:, at] + forcing[:, at]
        if j == 0:
            part = part + (new_first - first)
        if j == cells // 128 - 1:
            part = part + (new_final - final)
        send_ref[j, :64] = VALUE_SCALE * part
        send_ref[j, 64:] = CHANGE_SCALE * change_ref[...]


def whole(*shape):
    return pl.BlockSpec(memory_space=pltpu.VMEM)


def scalars():
    return pl.BlockSpec(memory_space=pltpu.SMEM)


def extent(shape):
    return getattr(shape, "shape", shape)


def call(kernel, shapes, places, args, name, room, cost=None):
    return pl.pallas_call(
        kernel,
        in_specs=[scalars()] * places + [whole()] * (len(args) - places),
        out_specs=[whole() if len(s) > 1 else scalars() for s in map(extent, shapes)],
        out_shape=[s if hasattr(s, "dtype") else jax.ShapeDtypeStruct(s, F32) for s in shapes],
        compiler_params=pltpu.CompilerParams(vmem_limit_bytes=room << 20),
        cost_estimate=cost,
        name=name,
    )(*args)


def exponent(v):
    return jnp.ceil(jnp.log2(jnp.maximum(v, 1e-30)))


def block_exponent(v):
    return exponent(jnp.max(jnp.abs(v), axis=(0, 1), keepdims=True))


def scaled(v, power):
    return v * jnp.exp2(15.0 - power)


def restored(v, power):
    return v * jnp.exp2(power - 15.0)


def tags(t, value_power, change_power):
    lane = lax.broadcasted_iota(jnp.int32, (8, 128), 1)
    power = exponent(jnp.abs(t))
    unit = t * jnp.exp2(-power)
    coarse = rounded(unit)
    fine = 256.0 * (unit - coarse)
    scales = jnp.where(lane < 112, value_power, change_power)
    return jnp.where(
        lane < 32, coarse, jnp.where(lane < 64, fine, jnp.where(lane < 96, power, scales))
    )


def read_tags(r):
    t = (r[:, :1] + r[:, 32:33] / 256.0) * jnp.exp2(r[:, 64:65])
    return t, r[:1, 96:97], r[:1, 112:113]


def put(ref, change, value, t):
    value_power, change_power = block_exponent(value), block_exponent(change)
    value = scaled(value, value_power)
    change = scaled(fold(change), change_power)
    extra = tags(t, value_power, change_power)
    for i in range(ref.shape[0]):
        ref[i, :64] = value
        ref[i, 64:96] = change
        ref[i, 96:] = extra


def take(r):
    t, value_power, change_power = read_tags(r[96:])
    return unfold(restored(r[64:96], change_power)), restored(r[:64], value_power), t


def join(earlier, later):
    change, offset = later
    wide = jnp.concatenate([earlier[1], earlier[0]], axis=1)
    moved = wide + mix(change, wide)
    return moved[:, 128:] + change, moved[:, :128] + offset


def near_kernel(r_ref, t_ref, other_ref, send_ref, value_ref, matrix_ref):
    count = r_ref.shape[0]
    spans = [
        (unfold(r_ref[j, 64:] / CHANGE_SCALE), r_ref[j, :64] / VALUE_SCALE) for j in range(count)
    ]
    before = [None] + spans[:1]
    pairs = [join(spans[j], spans[j + 1]) for j in range(0, count, 2)]
    upto = pairs[:1]
    if count == 8:
        quads = [join(pairs[0], pairs[1]), join(pairs[2], pairs[3])]
        total = join(quads[0], quads[1])
        upto = [pairs[0], quads[0], join(quads[0], pairs[2])]
    else:
        total = join(pairs[0], pairs[1])
    for i, span in enumerate(upto):
        before += [span, join(span, spans[2 * i + 2])]
    for j in range(count):
        matrix, value = before[j] if j else (jnp.zeros((64, 64), F32), jnp.zeros((64, 128), F32))
        value_ref[j] = value
        matrix_ref[j] = matrix
    put(send_ref, *total, t_ref[...] + other_ref[...])


def far_kernel(place_ref, r_ref, send_ref, value_ref, matrix_ref):
    count = r_ref.shape[0]
    me = place_ref[0]
    spans, traces = [], []
    for i in range(count):
        change, value, t = take(r_ref[i])
        spans.append((change, value))
        traces.append(t)
    upto = [(jnp.zeros((64, 64), F32), jnp.zeros((64, 128), F32)), spans[0]]
    upto.append(join(spans[0], spans[1]))
    if count == 4:
        upto.append(join(upto[2], spans[2]))
        upto.append(join(upto[2], join(spans[2], spans[3])))
    own = upto[0]
    before = total = mine = jnp.zeros((8, 1), F32)
    for i in range(count):
        own = tuple(jnp.where(me == i, new, old) for new, old in zip(upto[i], own))
        before = jnp.where(me == i, total, before)
        mine = jnp.where(me == i, traces[i], mine)
        total = total + traces[i]
    matrix_ref[...], value_ref[...] = own
    spread = jnp.sum(before, axis=0, keepdims=True)
    t = jnp.concatenate([total[:2], mine[:2], spread, jnp.zeros((3, 1), F32)], axis=0)
    put(send_ref, *upto[count], jnp.broadcast_to(t, (8, 128)))


def back_kernel(
    place_ref, strip_ref, r_ref, far_value, far_matrix, near_value, near_matrix, send_ref
):
    me, strip = place_ref[0], strip_ref[0]
    state = own = jnp.zeros((64, 128), F32)
    before = total = mine = jnp.zeros((8, 1), F32)
    copies = 2
    count = r_ref.shape[0] // copies
    for i in range(count):
        own = jnp.where(me == i, state, own)
        before = jnp.where(me == i, total, before)
        t = sum(read_tags(r_ref[copies * i + n, 96:])[0] for n in range(copies))
        mine = jnp.where(me == i, t, mine)
        total = total + t
        if i < count - 1:
            change, value, _ = take(r_ref[copies * i + strip])
            state = state + mix(change, state) + value if i else value
    entry = own + mix(far_matrix[...], own) + far_value[...]
    near = near_matrix.shape[0]
    states = mix(near_matrix[...].reshape(near * 64, 64), entry)
    spread = jnp.sum(before[:2], axis=0, keepdims=True)
    t = jnp.concatenate([mine[2:5], spread, jnp.zeros((4, 1), F32)], axis=0)
    t = jnp.broadcast_to(t, (8, 128))
    states = [entry + states[j * 64 : (j + 1) * 64] + near_value[j] for j in range(near)]
    power = block_exponent(functools.reduce(jnp.maximum, [jnp.abs(state) for state in states]))
    extra = tags(t, power, power)
    for j in range(near):
        send_ref[j, :64] = scaled(states[j], power)
        send_ref[j, 64:] = extra


def final_kernel(place_ref, me_ref, r_ref, g_ref, state_ref, log_ref):
    leading, me = place_ref[0] == 0, me_ref[0]
    count = r_ref.shape[0]
    earlier = jnp.zeros((1, 1), F32)
    own = jnp.zeros((8, 1), F32)
    for j in range(count):
        at = slice(j * 128, (j + 1) * 128)
        t, power, _ = read_tags(r_ref[j, 64:])
        state = restored(r_ref[j, :64], power)
        state_ref[0, 0, :, at] = jnp.where(leading, g_ref[0, 0, :, at], state)
        earlier = earlier + t[2:3] + t[3:4] + jnp.where(j < me, t[0:1] + t[1:2], 0.0)
        own = jnp.where(me == j, t, own)
    first = earlier + own[0:1]
    second = first + own[1:2]
    log_ref[0] = -(STEP / WIDTH) * first[0, 0]
    log_ref[1] = -(STEP / WIDTH) * second[0, 0]


def exchange(v, axes):
    return lax.all_to_all(v.astype(F16), axes, 0, 0, tiled=True).astype(F32)


def body(guess, kernels, biases, probes):
    strips = lax.axis_size(SPACE)
    strip = lax.axis_index(SPACE)
    near = lax.axis_size(NEAR)
    far, last = lax.axis_size("zh"), lax.axis_size("x")
    cells = guess.shape[3]
    place = lax.axis_index(TM).reshape(1)

    up, down, kernels = edges(guess, probes, kernels)
    forward = [(i, i + 1) for i in range(strips - 1)]
    backward = [(i + 1, i) for i in range(strips - 1)]
    low = lax.ppermute(down, SPACE, forward)
    high = lax.ppermute(up, SPACE, backward)
    state, offset, change, inner, pull, turned = call(
        inner_kernel,
        [
            (64, cells),
            (64, cells),
            (32, 128),
            (8, 128),
            (2, 64, cells),
            jax.ShapeDtypeStruct((128, 576), BF16),
        ],
        1,
        (place, guess, probes, kernels, biases),
        "inner",
        20,
        pl.CostEstimate(flops=450_000_000, bytes_accessed=2_000_000, transcendentals=65536),
    )
    send, trace = call(
        functools.partial(outer_kernel, strips),
        [(near, 96, 128), (8, 128)],
        1,
        (
            strip.reshape(1), guess, low, high, probes, kernels, biases,
            state, offset, change, inner, pull, turned,
        ),
        "outer",
        20,
    )
    got = exchange(send, NEAR)
    across = [(i, i ^ 1) for i in range(strips)]
    other = lax.ppermute(
        trace, SPACE, [((i + 1) % strips, (j + 1) % strips) for i, j in across]
    )
    send, near_value, near_matrix = call(
        near_kernel,
        [(far, 104, 128), (near, 64, 128), (near, 64, 64)],
        0,
        (got, trace, other),
        "near",
        8,
    )
    got = exchange(send, "zh")
    send, far_value, far_matrix = call(
        far_kernel,
        [(2 * last, 104, 128), (64, 128), (64, 64)],
        1,
        (lax.axis_index("zh").reshape(1), got),
        "far",
        8,
    )
    got = exchange(send, ("x", "sl"))
    (send,) = call(
        back_kernel,
        [(near, 72, 128)],
        2,
        (
            lax.axis_index("x").reshape(1),
            lax.axis_index("sl").reshape(1),
            got,
            far_value,
            far_matrix,
            near_value,
            near_matrix,
        ),
        "back",
        8,
    )
    got = exchange(send, NEAR)
    return call(
        final_kernel,
        [(1, 1, 64, cells), (2,)],
        2,
        (place, lax.axis_index(NEAR).reshape(1), got, guess),
        "final",
        8,
    )


def solution(mesh):
    finer = Mesh(
        mesh.devices.reshape(4, 4, 4, 2, 2, 2), ("x", "zh", "zl", "c", "sh", "sl")
    )
    placed = (
        P(TM, None, None, SPACE),
        P(TM, None, None),
        P(TM, None),
        P(None, None, None, SPACE),
    )
    return jax.shard_map(
        body,
        mesh=finer,
        in_specs=placed,
        out_specs=(P(TM, None, None, SPACE), P(TM)),
        check_vma=False,
    )
```

```python
import functools

import jax
import jax.numpy as jnp
from jax import lax
from jax.experimental import pallas as pl
from jax.experimental.pallas import tpu as pltpu
from jax.sharding import Mesh
from jax.sharding import PartitionSpec as P

WIDTH = 64
STEP = 0.0078125
TM = ("x", "zh", "zl", "c")
NEAR = ("zl", "c")
SPACE = ("sh", "sl")
VALUE_SCALE = 2048.0
CHANGE_SCALE = 32768.0
F16 = jnp.float16
F32 = jnp.float32
BF16 = jnp.bfloat16


def split3(m):
    hi = m.astype(BF16)
    return hi, (m - hi.astype(F32)).astype(BF16)


def left3(m):
    hi, lo = split3(m)
    return jnp.concatenate([hi, hi, lo], axis=1)


def right3(v):
    hi, lo = split3(v)
    return jnp.concatenate([hi, lo, hi], axis=0)


def mix(m, v):
    return jnp.dot(left3(m), right3(v), preferred_element_type=F32)


def fold(m):
    half = m.shape[0] // 2
    return jnp.concatenate([m[:half], m[half:]], axis=1)


def unfold(m):
    half = m.shape[1] // 2
    return jnp.concatenate([m[:, :half], m[:, half:]], axis=0)


def eye(n):
    return (
        lax.broadcasted_iota(jnp.int32, (n, n), 0) == lax.broadcasted_iota(jnp.int32, (n, n), 1)
    ).astype(F32)


def edge_kernel(
    g_ref, p_ref, k_ref, b_ref, up_ref, down_ref, kv_ref, bv_ref, p_first, p_last, sems
):
    end = g_ref.shape[3] - 128
    first, last = pl.ds(0, 128), pl.ds(end, 128)
    copies = [
        pltpu.make_async_copy(p_ref.at[:, 0, :, first], p_first, sems.at[0]),
        pltpu.make_async_copy(p_ref.at[:, 0, :, last], p_last, sems.at[1]),
        pltpu.make_async_copy(g_ref.at[0, 0, :, first], up_ref.at[pl.ds(0, 64)], sems.at[2]),
        pltpu.make_async_copy(g_ref.at[0, 0, :, last], down_ref.at[pl.ds(0, 64)], sems.at[3]),
        pltpu.make_async_copy(k_ref, kv_ref, sems.at[4]),
        pltpu.make_async_copy(b_ref, bv_ref, sems.at[5]),
    ]
    for copy in copies:
        copy.start()
    for copy in copies:
        copy.wait()
    up_ref[64:] = jnp.concatenate([p_first[n].astype(F32)[:, :WIDTH] for n in range(2)], axis=1)
    down_ref[64:] = jnp.concatenate([p_last[n].astype(F32)[:, WIDTH:] for n in range(2)], axis=1)


def edges(*args):
    held = [pltpu.with_memory_space_constraint(v, pltpu.HBM) for v in args]
    return pl.pallas_call(
        edge_kernel,
        in_specs=[pl.BlockSpec(memory_space=pltpu.HBM)] * 4,
        out_specs=[whole()] * 4,
        out_shape=[jax.ShapeDtypeStruct((128, 128), F32)] * 2
        + [jax.ShapeDtypeStruct(v.shape, v.dtype) for v in args[2:]],
        scratch_shapes=[pltpu.VMEM((2, 64, 128), BF16)] * 2 + [pltpu.SemaphoreType.DMA((6,))],
        compiler_params=pltpu.CompilerParams(vmem_limit_bytes=2 << 20),
        name="edges",
    )(*held)


def taps(v, closed=False):
    n = v.shape[1]
    column = lax.broadcasted_iota(jnp.int32, (16, n), 1) & (WIDTH - 1)
    keep = [jnp.where(column == edge, 0.0, 1.0).astype(BF16) for edge in (WIDTH - 1, 0)]
    keep = [jnp.concatenate([k] * (v.shape[0] // 16), axis=0) for k in keep]
    left = pltpu.roll(v * keep[0], 1, 1)
    right = pltpu.roll(v * keep[1], n - 1, 1)
    lane = lax.broadcasted_iota(jnp.int32, (v.shape[0], 128), 1)
    low = jnp.where(lane < WIDTH, 1.0, 0.0).astype(BF16)
    high = jnp.where(lane < WIDTH, 0.0, 1.0).astype(BF16)
    rows = []
    for part in (left, v, right):
        above = pltpu.roll(part, WIDTH, 1)
        below = jnp.concatenate([above[:, 128:], above[:, :128]], axis=1)
        if closed:
            above = jnp.concatenate([above[:, :128] * high, above[:, 128:]], axis=1)
            below = jnp.concatenate([below[:, : n - 128], below[:, n - 128 :] * low], axis=1)
        rows.append((above, part, below))
    return jnp.concatenate([rows[dx][dy] for dy in range(3) for dx in range(3)], axis=0)


def rounded(v):
    return v.astype(BF16).astype(F32)


def convolve(kernel, v, at=None):
    stack = taps(v.astype(BF16))
    return jnp.dot(kernel, stack if at is None else stack[:, at], preferred_element_type=F32)


def bias_of(b_ref, layer):
    return jnp.sum(
        jnp.where(eye(64) == 1.0, b_ref[layer : layer + 1, :], 0.0), axis=1, keepdims=True
    )


def adjoint(k_ref):
    blocks = []
    for at in range(0, 9 * 64, 128):
        both = jnp.concatenate([k_ref[n, :, at : at + 128].astype(F32) for n in range(2)], axis=0)
        turned = both.T
        blocks += [turned[i : i + 64] for i in range(0, turned.shape[0], 64)]
    blocks = blocks[::-1]
    return jnp.concatenate(
        [
            jnp.concatenate([block[:, n * 64 : (n + 1) * 64] for block in blocks], axis=1)
            for n in range(2)
        ],
        axis=0,
    ).astype(BF16)


def inner_kernel(
    place_ref, g_ref, p_ref, k_ref, b_ref, state_ref, offset_ref, change_ref, t_ref, pull_ref, a_ref
):
    leading = place_ref[0] == 0
    g = g_ref[0, 0]
    activation = jnp.tanh(g)
    slopes = 1.0 - activation * activation
    forcing = STEP * (convolve(k_ref[0], activation) + bias_of(b_ref, 0))
    turned = adjoint(k_ref)
    a_ref[...] = turned
    total = jnp.zeros(g.shape, F32)
    for n in range(2):
        probe = p_ref[n, 0]
        pulled = jnp.dot(turned, taps(probe, True), preferred_element_type=F32)
        total = total + pulled[:64] * rounded(slopes * probe.astype(F32))
        pull_ref[n] = pulled[64:]
    t_ref[...] = jnp.full((8, 128), 0.5 * jnp.sum(total))
    both = k_ref[0].astype(F32) + k_ref[1].astype(F32)
    pair = both[:, :128] + both[:, 128:256] + both[:, 256:384] + both[:, 384:512]
    coarse = STEP * (pair[:, :64] + pair[:, 64:] + both[:, 512:])
    state_ref[...] = g + forcing
    offset_ref[...] = forcing + jnp.where(leading, g, -mix(coarse, g))
    change_ref[...] = fold(jnp.where(leading, -eye(64), coarse))


def sides(v):
    column = lax.broadcasted_iota(jnp.int32, v.shape, 1) & (WIDTH - 1)
    left = pltpu.roll(jnp.where(column == WIDTH - 1, 0.0, v), 1, 1)
    right = pltpu.roll(jnp.where(column == 0, 0.0, v), v.shape[1] - 1, 1)
    return jnp.concatenate([left, v, right], axis=0).astype(BF16)


def twice(v, at):
    return jnp.concatenate([v[:, at : at + WIDTH]] * 2, axis=1)


def outer_kernel(
    strips,
    strip_ref,
    g_ref,
    low_ref,
    high_ref,
    p_ref,
    k_ref,
    b_ref,
    state_ref,
    offset_ref,
    change_ref,
    inner_ref,
    pull_ref,
    a_ref,
    send_ref,
    t_ref,
):
    cells = state_ref.shape[1]
    last = cells - 128
    ends = jnp.concatenate(
        [low_ref[:64], g_ref[0, 0, :, :128], g_ref[0, 0, :, last:], high_ref[:64]], axis=1
    )
    probe_mid = [p_ref[n, 0].astype(F32) for n in range(2)]
    activation = jnp.tanh(ends)
    end_slopes = 1.0 - activation * activation
    forcing = STEP * (convolve(k_ref[0], activation) + bias_of(b_ref, 0))

    turned = a_ref[...]
    pulls = [
        jnp.dot(turned[:, :192], sides(low_ref[64:]), preferred_element_type=F32),
        jnp.dot(turned[:, 384:], sides(high_ref[64:]), preferred_element_type=F32),
    ]
    edge_probe = [
        jnp.concatenate([v[:, :WIDTH] for v in probe_mid], axis=1),
        jnp.concatenate([v[:, cells - WIDTH :] for v in probe_mid], axis=1),
    ]
    total = sum(
        pulls[i][:64] * rounded(twice(end_slopes, (128, 320)[i]) * edge_probe[i]) for i in range(2)
    )
    trace = inner_ref[...] + 0.5 * jnp.sum(total)

    lane = lax.broadcasted_iota(jnp.int32, (64, 128), 1)
    fresh = ends + forcing
    first, final = state_ref[:, :128], state_ref[:, last:]
    new_first = jnp.where(lane < WIDTH, fresh[:, 128:256], first)
    new_final = jnp.where(lane < WIDTH, final, fresh[:, 256:384])
    current = jnp.concatenate(
        [fresh[:, :128], new_first, state_ref[:, 128:last], new_final, fresh[:, 384:]], axis=1
    )
    wide = cells + 256
    far_lane = lax.broadcasted_iota(jnp.int32, (64, wide), 1)
    outside = ((strip_ref[0] == 0) & (far_lane < 128)) | (
        (strip_ref[0] == strips - 1) & (far_lane >= wide - 128)
    )
    activation = jnp.where(outside, 0.0, jnp.tanh(current))
    forcing = convolve(k_ref[1], activation, slice(128, 128 + cells))
    forcing = STEP * (forcing + bias_of(b_ref, 1))
    middle = activation[:, 128 : 128 + cells]
    slopes = 1.0 - middle * middle
    total = sum(pull_ref[n] * rounded(slopes * probe_mid[n]) for n in range(2))
    edge = sum(
        pulls[i][64:] * rounded(twice(slopes, (0, cells - WIDTH)[i]) * edge_probe[i])
        for i in range(2)
    )
    rows = lax.broadcasted_iota(jnp.int32, (8, 128), 0)
    second = 0.5 * (jnp.sum(total) + jnp.sum(edge))
    t_ref[...] = jnp.where(rows == 1, second, jnp.where(rows == 0, trace, 0.0))
    for j in range(cells // 128):
        at = slice(j * 128, (j + 1) * 128)
        part = offset_ref[:, at] + forcing[:, at]
        if j == 0:
            part = part + (new_first - first)
        if j == cells // 128 - 1:
            part = part + (new_final - final)
        send_ref[j, :64] = VALUE_SCALE * part
        send_ref[j, 64:] = CHANGE_SCALE * change_ref[...]


def whole(*shape):
    return pl.BlockSpec(memory_space=pltpu.VMEM)


def scalars():
    return pl.BlockSpec(memory_space=pltpu.SMEM)


def extent(shape):
    return getattr(shape, "shape", shape)


def call(kernel, shapes, places, args, name, room, cost=None):
    return pl.pallas_call(
        kernel,
        in_specs=[scalars()] * places + [whole()] * (len(args) - places),
        out_specs=[whole() if len(s) > 1 else scalars() for s in map(extent, shapes)],
        out_shape=[s if hasattr(s, "dtype") else jax.ShapeDtypeStruct(s, F32) for s in shapes],
        compiler_params=pltpu.CompilerParams(vmem_limit_bytes=room << 20),
        cost_estimate=cost,
        name=name,
    )(*args)


def exponent(v):
    return jnp.ceil(jnp.log2(jnp.maximum(v, 1e-30)))


def block_exponent(v):
    return exponent(jnp.max(jnp.abs(v), axis=(0, 1), keepdims=True))


def scaled(v, power):
    return v * jnp.exp2(15.0 - power)


def restored(v, power):
    return v * jnp.exp2(power - 15.0)


def tags(t, value_power, change_power):
    lane = lax.broadcasted_iota(jnp.int32, (8, 128), 1)
    power = exponent(jnp.abs(t))
    unit = t * jnp.exp2(-power)
    coarse = rounded(unit)
    fine = 256.0 * (unit - coarse)
    scales = jnp.where(lane < 112, value_power, change_power)
    return jnp.where(
        lane < 32, coarse, jnp.where(lane < 64, fine, jnp.where(lane < 96, power, scales))
    )


def read_tags(r):
    t = (r[:, :1] + r[:, 32:33] / 256.0) * jnp.exp2(r[:, 64:65])
    return t, r[:1, 96:97], r[:1, 112:113]


def put(ref, change, value, t):
    value_power, change_power = block_exponent(value), block_exponent(change)
    value = scaled(value, value_power)
    change = scaled(fold(change), change_power)
    extra = tags(t, value_power, change_power)
    for i in range(ref.shape[0]):
        ref[i, :64] = value
        ref[i, 64:96] = change
        ref[i, 96:] = extra


def take(r):
    t, value_power, change_power = read_tags(r[96:])
    return unfold(restored(r[64:96], change_power)), restored(r[:64], value_power), t


def join(earlier, later):
    change, offset = later
    wide = jnp.concatenate([earlier[1], earlier[0]], axis=1)
    moved = wide + mix(change, wide)
    return moved[:, 128:] + change, moved[:, :128] + offset


def near_kernel(r_ref, t_ref, other_ref, send_ref, value_ref, matrix_ref):
    count = r_ref.shape[0]
    spans = [
        (unfold(r_ref[j, 64:] / CHANGE_SCALE), r_ref[j, :64] / VALUE_SCALE) for j in range(count)
    ]
    before = [None] + spans[:1]
    pairs = [join(spans[j], spans[j + 1]) for j in range(0, count, 2)]
    upto = pairs[:1]
    if count == 8:
        quads = [join(pairs[0], pairs[1]), join(pairs[2], pairs[3])]
        total = join(quads[0], quads[1])
        upto = [pairs[0], quads[0], join(quads[0], pairs[2])]
    else:
        total = join(pairs[0], pairs[1])
    for i, span in enumerate(upto):
        before += [span, join(span, spans[2 * i + 2])]
    for j in range(count):
        matrix, value = before[j] if j else (jnp.zeros((64, 64), F32), jnp.zeros((64, 128), F32))
        value_ref[j] = value
        matrix_ref[j] = matrix
    put(send_ref, *total, t_ref[...] + other_ref[...])


def far_kernel(place_ref, r_ref, send_ref, value_ref, matrix_ref):
    count = r_ref.shape[0]
    me = place_ref[0]
    spans, traces = [], []
    for i in range(count):
        change, value, t = take(r_ref[i])
        spans.append((change, value))
        traces.append(t)
    upto = [(jnp.zeros((64, 64), F32), jnp.zeros((64, 128), F32)), spans[0]]
    upto.append(join(spans[0], spans[1]))
    if count == 4:
        upto.append(join(upto[2], spans[2]))
        upto.append(join(upto[2], join(spans[2], spans[3])))
    own = upto[0]
    before = total = mine = jnp.zeros((8, 1), F32)
    for i in range(count):
        own = tuple(jnp.where(me == i, new, old) for new, old in zip(upto[i], own))
        before = jnp.where(me == i, total, before)
        mine = jnp.where(me == i, traces[i], mine)
        total = total + traces[i]
    matrix_ref[...], value_ref[...] = own
    spread = jnp.sum(before, axis=0, keepdims=True)
    t = jnp.concatenate([total[:2], mine[:2], spread, jnp.zeros((3, 1), F32)], axis=0)
    put(send_ref, *upto[count], jnp.broadcast_to(t, (8, 128)))


def back_kernel(
    place_ref, strip_ref, r_ref, far_value, far_matrix, near_value, near_matrix, send_ref
):
    me, strip = place_ref[0], strip_ref[0]
    state = own = jnp.zeros((64, 128), F32)
    before = total = mine = jnp.zeros((8, 1), F32)
    copies = 2
    count = r_ref.shape[0] // copies
    for i in range(count):
        own = jnp.where(me == i, state, own)
        before = jnp.where(me == i, total, before)
        t = sum(read_tags(r_ref[copies * i + n, 96:])[0] for n in range(copies))
        mine = jnp.where(me == i, t, mine)
        total = total + t
        if i < count - 1:
            change, value, _ = take(r_ref[copies * i + strip])
            state = state + mix(change, state) + value if i else value
    entry = own + mix(far_matrix[...], own) + far_value[...]
    near = near_matrix.shape[0]
    states = mix(near_matrix[...].reshape(near * 64, 64), entry)
    spread = jnp.sum(before[:2], axis=0, keepdims=True)
    t = jnp.concatenate([mine[2:5], spread, jnp.zeros((4, 1), F32)], axis=0)
    t = jnp.broadcast_to(t, (8, 128))
    states = [entry + states[j * 64 : (j + 1) * 64] + near_value[j] for j in range(near)]
    power = block_exponent(functools.reduce(jnp.maximum, [jnp.abs(state) for state in states]))
    extra = tags(t, power, power)
    for j in range(near):
        send_ref[j, :64] = scaled(states[j], power)
        send_ref[j, 64:] = extra


def final_kernel(place_ref, me_ref, r_ref, g_ref, state_ref, log_ref):
    leading, me = place_ref[0] == 0, me_ref[0]
    count = r_ref.shape[0]
    earlier = jnp.zeros((1, 1), F32)
    own = jnp.zeros((8, 1), F32)
    for j in range(count):
        at = slice(j * 128, (j + 1) * 128)
        t, power, _ = read_tags(r_ref[j, 64:])
        state = restored(r_ref[j, :64], power)
        state_ref[0, 0, :, at] = jnp.where(leading, g_ref[0, 0, :, at], state)
        earlier = earlier + t[2:3] + t[3:4] + jnp.where(j < me, t[0:1] + t[1:2], 0.0)
        own = jnp.where(me == j, t, own)
    first = earlier + own[0:1]
    second = first + own[1:2]
    log_ref[0] = -(STEP / WIDTH) * first[0, 0]
    log_ref[1] = -(STEP / WIDTH) * second[0, 0]


def exchange(v, axes):
    return lax.all_to_all(v.astype(F16), axes, 0, 0, tiled=True).astype(F32)


def body(guess, kernels, biases, probes):
    strips = lax.axis_size(SPACE)
    strip = lax.axis_index(SPACE)
    near = lax.axis_size(NEAR)
    far, last = lax.axis_size("zh"), lax.axis_size("x")
    cells = guess.shape[3]
    place = lax.axis_index(TM).reshape(1)

    up, down, kernels, biases = edges(guess, probes, kernels, biases)
    forward = [(i, i + 1) for i in range(strips - 1)]
    backward = [(i + 1, i) for i in range(strips - 1)]
    low = lax.ppermute(down, SPACE, forward)
    high = lax.ppermute(up, SPACE, backward)
    state, offset, change, inner, pull, turned = call(
        inner_kernel,
        [
            (64, cells),
            (64, cells),
            (32, 128),
            (8, 128),
            (2, 64, cells),
            jax.ShapeDtypeStruct((128, 576), BF16),
        ],
        1,
        (place, guess, probes, kernels, biases),
        "inner",
        20,
        pl.CostEstimate(flops=450_000_000, bytes_accessed=2_000_000, transcendentals=65536),
    )
    send, trace = call(
        functools.partial(outer_kernel, strips),
        [(near, 96, 128), (8, 128)],
        1,
        (
            strip.reshape(1), guess, low, high, probes, kernels, biases,
            state, offset, change, inner, pull, turned,
        ),
        "outer",
        20,
    )
    got = exchange(send, NEAR)
    across = [(i, i ^ 1) for i in range(strips)]
    other = lax.ppermute(
        trace, SPACE, [((i + 1) % strips, (j + 1) % strips) for i, j in across]
    )
    send, near_value, near_matrix = call(
        near_kernel,
        [(far, 104, 128), (near, 64, 128), (near, 64, 64)],
        0,
        (got, trace, other),
        "near",
        8,
    )
    got = exchange(send, "zh")
    send, far_value, far_matrix = call(
        far_kernel,
        [(2 * last, 104, 128), (64, 128), (64, 64)],
        1,
        (lax.axis_index("zh").reshape(1), got),
        "far",
        8,
    )
    got = exchange(send, ("x", "sl"))
    (send,) = call(
        back_kernel,
        [(near, 72, 128)],
        2,
        (
            lax.axis_index("x").reshape(1),
            lax.axis_index("sl").reshape(1),
            got,
            far_value,
            far_matrix,
            near_value,
            near_matrix,
        ),
        "back",
        8,
    )
    got = exchange(send, NEAR)
    return call(
        final_kernel,
        [(1, 1, 64, cells), (2,)],
        2,
        (place, lax.axis_index(NEAR).reshape(1), got, guess),
        "final",
        8,
    )


def solution(mesh):
    finer = Mesh(
        mesh.devices.reshape(4, 4, 4, 2, 2, 2), ("x", "zh", "zl", "c", "sh", "sl")
    )
    placed = (
        P(TM, None, None, SPACE),
        P(TM, None, None),
        P(TM, None),
        P(None, None, None, SPACE),
    )
    return jax.shard_map(
        body,
        mesh=finer,
        in_specs=placed,
        out_specs=(P(TM, None, None, SPACE), P(TM)),
        check_vma=False,
    )
```
